32 devices in a mesh: seq: 4 (over x, core), dp: 8 (over z, y).
Axes of the slice: x: 2, y: 2, z: 4, core: 2. Of those that a mesh axis runs over, the one named last changes fastest.
Arguments:
- tokens: bfloat16 [8, 2048, 2048], P('dp', 'seq'), may hold values from -6 to 6
- log_decay: float32 [8, 8, 2048], P('dp', None, 'seq'), may hold values from -1 to 0
- w_qkv: bfloat16 [2048, 3072], P('dp'), may hold values from -0.125 to 0.125
- w_gate: bfloat16 [2048, 1024], P('dp'), may hold values from -0.125 to 0.125
- w_out: bfloat16 [1024, 2048], P('dp'), may hold values from -0.1875 to 0.1875
- norm_gain: float32 [1024], replicated, may hold values from 0.1 to 1.9
Outputs:
- mixed_rows: bfloat16 [8, 2048, 2048], P('dp', 'seq')
The draws below stay inside these ranges and needn't reach their ends.
All inputs are finite; a program needn't handle non-finite values.
Results may differ from the reference program's by a relative error of at most 0.0065.
Values may be sent and summed in bfloat16 or wider, within the bound.
A program may use at most 64 MiB of HBM per device.

```python
import math
import jax
import jax.numpy as jnp
from jax import lax

D = 2048
HEAD_TOTAL = 8
HEAD_DIM = 128
TOK_DEV = 512
SEQUENCE_LENGTH = 2048
SEQUENCE_TOTAL = 8
N_SEQ = 4


def draw_log_decay(key, part):
    key_vectors = jax.random.split(key, 6)
    head_draw = jax.random.uniform(key_vectors[0], (SEQUENCE_TOTAL, HEAD_TOTAL, 1), jnp.float32)
    class_draw = jax.random.uniform(key_vectors[1], (SEQUENCE_TOTAL, HEAD_TOTAL, 1), jnp.float32)
    fast_share = 0.5
    slow_low = math.log(0.05 * math.log(10.0) / SEQUENCE_LENGTH)
    slow_high = math.log(0.4 * math.log(10.0) / SEQUENCE_LENGTH)
    slow_rate = jnp.exp(slow_low + head_draw * (slow_high - slow_low))
    fast_rate = jnp.exp(math.log(1.0 / 50.0) + head_draw * math.log(2.0))
    decay_speed = jnp.where(class_draw < fast_share, fast_rate, slow_rate)
    position_multiplier = jnp.exp(jax.random.uniform(key_vectors[2], (SEQUENCE_TOTAL, HEAD_TOTAL, SEQUENCE_LENGTH), jnp.float32, -0.5, 0.5))
    block_multiplier = jax.random.uniform(key_vectors[3], (SEQUENCE_TOTAL, HEAD_TOTAL, SEQUENCE_LENGTH // TOK_DEV, 1), jnp.float32, 0.5, 1.5)
    block_multiplier = jnp.broadcast_to(block_multiplier, (SEQUENCE_TOTAL, HEAD_TOTAL, SEQUENCE_LENGTH // TOK_DEV, TOK_DEV)).reshape(SEQUENCE_TOTAL, HEAD_TOTAL, SEQUENCE_LENGTH)
    spike_sample = jax.random.uniform(key_vectors[4], (SEQUENCE_TOTAL, HEAD_TOTAL, SEQUENCE_LENGTH), jnp.float32)
    spike_penalty = jax.random.uniform(key_vectors[5], (SEQUENCE_TOTAL, HEAD_TOTAL, SEQUENCE_LENGTH), jnp.float32, math.log(0.5), math.log(0.8))
    spike_events = jnp.where(spike_sample < 2.0 / SEQUENCE_LENGTH, spike_penalty, 0.0)
    return (-decay_speed * position_multiplier * block_multiplier + spike_events).astype(jnp.float32)


def block_levels(stream_key, dims, pieces, smallest, high):
    loudness, own = 1.0, jax.random.fold_in(stream_key, 6)
    for position, blocks in pieces:
        steps = jnp.exp(jax.random.uniform(jax.random.fold_in(own, position), (blocks,), jnp.float32, smallest / len(pieces), high / len(pieces)))
        loudness = loudness * jnp.repeat(steps, dims[position] // blocks).reshape([-1 if axis == position else 1 for axis in range(len(dims))])
    return loudness


def noise(key, shape, deviation, limit, shards=(), kind=jnp.bfloat16):
    drawn = deviation * jax.random.normal(key, shape, jnp.float32)
    if shards:
        drawn = drawn * block_levels(key, shape, shards, -0.22, 0.18)
    return jnp.clip(drawn, -limit, limit).astype(kind)


def setup_inputs(seed: int = 0) -> dict:
    keys = jax.random.split(jax.random.key(seed), 7)
    return {
        "tokens": noise(keys[0], (SEQUENCE_TOTAL, SEQUENCE_LENGTH, D), 1.0, 6.0, ((0, 8), (1, 4))),
        "log_decay": draw_log_decay(jax.random.fold_in(keys[6], 71), 0),
        "w_qkv": noise(keys[2], (D, 3 * HEAD_TOTAL * HEAD_DIM), D ** -0.5, 0.125, ((0, 8),)),
        "w_gate": noise(keys[3], (D, HEAD_TOTAL * HEAD_DIM), D ** -0.5, 0.125, ((0, 8),)),
        "w_out": noise(keys[4], (HEAD_TOTAL * HEAD_DIM, D), (HEAD_TOTAL * HEAD_DIM) ** -0.5, 0.1875, ((0, 8),)),
        "norm_gain": jnp.clip(1.0 + 0.18 * jax.random.normal(keys[5], (HEAD_TOTAL * HEAD_DIM,), jnp.float32), 0.1, 1.9),
    }


def block_pass(tok_rows, decay_rows, carried, w_qkv, w_gate, w_out, norm_gain):
    tok_count = tok_rows.shape[0]
    projected = jnp.dot(tok_rows, w_qkv, preferred_element_type=jnp.float32)
    gate_pre = jnp.dot(tok_rows, w_gate, preferred_element_type=jnp.float32)
    activated = jax.nn.silu(projected).astype(jnp.bfloat16).reshape(tok_count, 3, HEAD_TOTAL, HEAD_DIM)
    query_rows = activated[:, 0].astype(jnp.float32)
    key_rows = activated[:, 1].astype(jnp.float32)
    value_rows = activated[:, 2].astype(jnp.float32)
    cum_decay = jnp.cumsum(decay_rows, axis=1)
    block_decay = cum_decay[:, -1]
    scores = jnp.einsum('thd,shd->hts', query_rows, key_rows)
    positions = jnp.arange(tok_count, dtype=jnp.int32)
    causal_mask = (positions[None, :] <= positions[:, None])[None, :, :]
    decay_gap = cum_decay[:, :, None] - cum_decay[:, None, :]
    decay_mat = jnp.where(causal_mask, jnp.exp(jnp.where(causal_mask, decay_gap, 0.0)), 0.0)
    weighted = (scores * decay_mat).astype(jnp.bfloat16)
    intra_part = jnp.einsum('hts,shd->thd', weighted.astype(jnp.float32), value_rows)
    key_factor = jnp.exp(block_decay[:, None] - cum_decay).T
    scaled_key = (key_rows * key_factor[:, :, None]).astype(jnp.bfloat16)
    local_state = jnp.einsum('thd,the->hde', scaled_key.astype(jnp.float32), value_rows)
    query_scaled = query_rows * jnp.exp(cum_decay).T[:, :, None]
    inter_part = jnp.einsum('thd,hde->the', query_scaled, carried, precision=lax.Precision.HIGHEST)
    attended = (intra_part + inter_part).reshape(tok_count, HEAD_TOTAL * HEAD_DIM)
    mean_square = lax.optimization_barrier(jnp.mean(attended * attended, axis=1, keepdims=True))
    normed = attended * lax.rsqrt(mean_square + 1e-06) * norm_gain
    gated = (normed * jax.nn.sigmoid(gate_pre)).astype(jnp.bfloat16)
    mixed_rows = jnp.dot(gated, w_out, preferred_element_type=jnp.float32).astype(jnp.bfloat16)
    new_state = jnp.exp(block_decay)[:, None, None] * carried + local_state
    return (mixed_rows, new_state)

def reference(tokens, log_decay, w_qkv, w_gate, w_out, norm_gain):

    def one_sequence(seq_items):
        seq_rows, seq_decay = seq_items
        blocks = seq_rows.reshape(N_SEQ, TOK_DEV, D)
        decays = seq_decay.reshape(HEAD_TOTAL, N_SEQ, TOK_DEV).transpose(1, 0, 2)

        def advance(carried, block_items):
            mixed_rows, new_state = block_pass(block_items[0], block_items[1], carried, w_qkv, w_gate, w_out, norm_gain)
            return (new_state, mixed_rows)
        first_state = jnp.zeros((HEAD_TOTAL, HEAD_DIM, HEAD_DIM), jnp.float32)
        final_state, outputs = lax.scan(advance, first_state, (blocks, decays))
        return outputs.reshape(SEQUENCE_LENGTH, D)
    return lax.map(one_sequence, (tokens, log_decay))
```

```python
import functools

import jax
import jax.numpy as jnp
from jax import lax
from jax.experimental import pallas as pl
from jax.experimental.pallas import tpu as pltpu
from jax.sharding import PartitionSpec as P

MESH = pl.DeviceIdType.MESH
F32 = jnp.float32
BF16 = jnp.bfloat16
PARTS = 4
WPIECES = 4
OPIECES = 2


def fused(n_dp, n_seq, tok_hbm, ld, gain, wqkv, wgate, wout, out,
          tok, tokp, W, WO, acc0, acc1, q_s, k_s, v_s, att, ccol, crow, cums, ldp, tot, st, cin,
          cout, ss, ssrow, ssin, gated, gsend,
          loc_sem, tok_sem, wr, ws, wpr, wps, orr, ors, opr, ops, tr, ts, lr, ls, tor, tos,
          str_, sts, gr, gs, ssr, sss, cr, cs):
    T, D = tok_hbm.shape
    H = ld.shape[0]
    F = gain.shape[1]
    hd = F // H
    HX = H // 2
    FX = F // 2
    N = n_dp
    K = N // 2
    R = D // N
    RO = F // N
    groups = n_seq // 4
    s = lax.axis_index("seq")
    d = lax.axis_index("dp")
    core = s % 2
    x = (s // 2) % 2
    group = s // 4
    partner = s + 1 - 2 * core
    xpeer = s + 2 - 4 * x

    def pos_of(i):
        return jnp.where(i % 2 == 0, i // 2, N - 1 - i // 2)

    def dev_at(p):
        p = lax.rem(p + 2 * N, N)
        return jnp.where(p < K, 2 * p, 2 * (N - 1 - p) + 1)

    pos = pos_of(d)
    ring_to = (dev_at(pos + 1), dev_at(pos - 1))

    def origin(dr, k):
        return dev_at(pos - k) if dr == 0 else dev_at(pos + k)

    def dev(seq=None, dp=None):
        return {"seq": s if seq is None else seq, "dp": d if dp is None else dp}

    def mk(src, dst, ssem, rsem, to):
        return pltpu.make_async_remote_copy(
            src_ref=src, dst_ref=dst, send_sem=ssem, recv_sem=rsem,
            device_id=to, device_id_type=MESH)

    npiece = (WPIECES, OPIECES)
    ring_sems = ((ws, wr, wps, wpr), (ors, orr, ops, opr))

    def piece(ph, dr, k, c, p):
        rows, buf = ((R, W), (RO, WO))[ph]
        width = buf.shape[1] // npiece[ph]
        q = rows // 2
        row = pl.multiple_of(origin(dr, k) * rows + c * q, q)
        return buf.at[pl.ds(row, q), pl.ds(p * width, width)]

    def has(ph, dr, k, p):
        return k < K or (k == K and (p * 2) // npiece[ph] == dr)

    def ring_desc(ph, dr, k, at, p):
        a, b = ring_sems[ph][:2]
        ref = piece(ph, dr, at, core, p)
        return mk(ref, ref, a.at[dr, p, k - 1], b.at[dr, p, k - 1], dev(dp=ring_to[dr]))

    def part_desc(ph, dr, k, c, p):
        a, b = ring_sems[ph][2:]
        ref = piece(ph, dr, k, c, p)
        return mk(ref, ref, a.at[dr, p, k - 1], b.at[dr, p, k - 1], dev(seq=partner))

    def begin(ph):
        for p in range(npiece[ph]):
            for dr in (0, 1):
                if has(ph, dr, 1, p):
                    ring_desc(ph, dr, 1, 0, p).start()

    def relay(ph, k, p):
        for dr in (0, 1):
            if not has(ph, dr, k, p):
                continue
            ring_desc(ph, dr, k, k, p).wait_recv()
            if has(ph, dr, k + 1, p):
                ring_desc(ph, dr, k + 1, k, p).start()
            part_desc(ph, dr, k, core, p).start()

    def collect(ph, k):
        for dr in (0, 1):
            for p in range(npiece[ph]):
                if has(ph, dr, k, p):
                    part_desc(ph, dr, k, 1 - core, p).wait_recv()

    def drain(ph):
        for k in range(1, K + 1):
            for dr in (0, 1):
                for p in range(npiece[ph]):
                    if has(ph, dr, k, p):
                        ring_desc(ph, dr, k, k, p).wait_send()
                        part_desc(ph, dr, k, core, p).wait_send()

    order = [d] + [origin(dr, k) for k in range(1, K) for dr in (0, 1)] + [origin(0, K)]

    def tok_desc(j):
        cols = pl.ds(pl.multiple_of(order[j] * R, R), R)
        return mk(tok_hbm.at[:, cols], tokp.at[:, cols], ts.at[j], tr.at[j], dev(seq=xpeer))

    def blk(b):
        return 2 * (x if b == 0 else 1 - x) + core

    def st_desc(b, i, mine):
        ref = st.at[blk(b) if mine else blk(b) + 1 - 2 * core, i]
        return mk(ref, ref, sts.at[b, i], str_.at[b, i], dev(seq=partner))

    def tot_desc(b, mine):
        ref = tot.at[blk(b) if mine else blk(b) + 1 - 2 * core]
        return mk(ref, ref, tos.at[b], tor.at[b], dev(seq=partner))

    def g_desc(i, mine):
        c = (x if mine else 1 - x) * FX + i * hd
        return mk(gsend.at[i], gated.at[:, pl.ds(pl.multiple_of(c, hd), hd)],
                  gs.at[i], gr.at[i], dev(seq=xpeer))

    ld_copy = mk(ld, ldp, ls, lr, dev(seq=xpeer))
    ss_copy = mk(ssrow.at[1], ssin, sss, ssr, dev(seq=xpeer))

    def chain_desc(i, to):
        return mk(cout.at[i], cin.at[i], cs.at[i], cr.at[i], dev(seq=to))

    base = pl.multiple_of(d * R, R)
    xcol = pl.multiple_of(x * FX, FX)
    loads = []
    for p in range(PARTS):
        src = wgate.at[:, pl.ds(xcol, FX)] if p == 3 else wqkv.at[:, pl.ds(p * F + xcol, FX)]
        loads.append(pltpu.make_async_copy(
            src, W.at[pl.ds(base, R), pl.ds(p * FX, FX)], loc_sem.at[p]))
    loads.append(pltpu.make_async_copy(
        wout, WO.at[pl.ds(pl.multiple_of(d * RO, RO), RO), :], loc_sem.at[4]))
    for c in loads:
        c.start()
    tok_load = pltpu.make_async_copy(tok_hbm, tok, tok_sem)
    tok_load.start()

    barrier = pltpu.get_barrier_semaphore()
    for who in (dev(dp=ring_to[0]), dev(dp=ring_to[1]), dev(seq=partner), dev(seq=xpeer)):
        pl.semaphore_signal(barrier, inc=1, device_id=who, device_id_type=MESH)
    greeted = 4
    if groups > 1:
        @pl.when(group > 0)
        def _():
            pl.semaphore_signal(barrier, inc=1, device_id=dev(seq=s - 4), device_id_type=MESH)

        @pl.when(group < groups - 1)
        def _():
            pl.semaphore_signal(barrier, inc=1, device_id=dev(seq=s + 4), device_id_type=MESH)
        greeted = greeted + jnp.where(group > 0, 1, 0) + jnp.where(group < groups - 1, 1, 0)
    for c in loads:
        c.wait()
    pl.semaphore_wait(barrier, greeted)

    begin(0)
    ld_copy.start()
    tok_desc(0).start()
    tok_desc(1).start()

    lane = lax.broadcasted_iota(jnp.int32, (H, T), 1)

    def decays(b, rows):
        cum = rows
        step = 1
        while step < T:
            cum = cum + jnp.where(lane >= step, pltpu.roll(cum, step, 1), 0.0)
            step *= 2
        cums[b] = cum
        for i in range(HX):
            row = cums[b, pl.ds(x * HX + i, 1), :]
            crow[b, i] = jnp.broadcast_to(row, (8, T))
            col = jnp.broadcast_to(row, (hd, T)).T
            ccol[b, i] = col
            tot[blk(b), i:i + 1, :] = col[T - 1:T, :]
        tot_desc(b, True).start()

    toks = (tok, tokp)
    accs = (acc0, acc1)
    tile = 512 if W.shape[1] % 512 == 0 else W.shape[1]

    def matmul(b, origins, first=False):
        rows = [pl.ds(pl.multiple_of(o * R, R), R) for o in origins]

        @pl.loop(0, W.shape[1] // tile)
        def _(j):
            cols = pl.ds(pl.multiple_of(j * tile, tile), tile)
            y = None
            for r in rows:
                z = jnp.dot(toks[b][:, r], W[r, cols], preferred_element_type=F32)
                y = z if y is None else y + z
            if first:
                accs[b][:, cols] = y
            else:
                accs[b][:, cols] += y

    def step_origins(k):
        return [origin(0, k)] if k == K else [origin(0, k), origin(1, k)]

    def silu(v):
        return (v / (1.0 + jnp.exp(-v))).astype(BF16)

    def head_local(b, i):
        a = accs[b]
        kk = silu(a[:, FX + i * hd:FX + (i + 1) * hd])
        vv = silu(a[:, 2 * FX + i * hd:2 * FX + (i + 1) * hd])
        k_s[b, i] = kk
        v_s[b, i] = vv
        q_s[b, i] = silu(a[:, i * hd:(i + 1) * hd])
        c = ccol[b, i]
        sk = (kk.astype(F32) * jnp.exp(c[T - 1:T, :] - c)).astype(BF16)
        st[blk(b), i] = lax.dot_general(sk, vv, (((0,), (0,)), ((), ())),
                                        preferred_element_type=F32)
        st_desc(b, i, True).start()

    half = T // 2
    tri = (lax.broadcasted_iota(jnp.int32, (half, half), 1)
           <= lax.broadcasted_iota(jnp.int32, (half, half), 0))

    def head_attend(b, i):
        for u in (0, 1):
            r = slice(u * half, (u + 1) * half)
            q = q_s[b, i, r, :]
            c = jnp.concatenate([ccol[b, i, r, :]] * (half // hd), axis=1)
            total = None
            for e in range(u + 1):
                z = slice(e * half, (e + 1) * half)
                sc = lax.dot_general(q, k_s[b, i, z, :], (((1,), (1,)), ((), ())),
                                     preferred_element_type=F32)
                gap = c - crow[b, i, 0:1, z]
                if e == u:
                    gap = jnp.where(tri, gap, -1e30)
                w = (sc * jnp.exp(gap)).astype(BF16)
                y = jnp.dot(w, v_s[b, i, z, :], preferred_element_type=F32)
                total = y if total is None else total + y
            att[b, i, r, :] = total

    def fold(first, count, i):
        def one(j, c):
            return jnp.exp(tot[j, i:i + 1, :]) * c + st[j, i]
        return lax.fori_loop(0, count, one, first)

    def head_final(b, i):
        first = cin[i]
        carried = fold(first, blk(b), i).astype(BF16)
        inter = jnp.dot(q_s[b, i], carried, preferred_element_type=F32)
        a = att[b, i] + inter * jnp.exp(ccol[b, i])
        if i == 0:
            ss[b] = a * a
        else:
            ss[b] += a * a
        g = accs[b][:, 3 * FX + i * hd:3 * FX + (i + 1) * hd]
        f = pl.ds(pl.multiple_of(x * FX + i * hd, hd), hd)
        val = (a * gain[:, f] * (1.0 / (1.0 + jnp.exp(-g)))).astype(BF16)
        if b == 0:
            gated[:, f] = val
        else:
            gsend[i] = val
            g_desc(i, True).start()

    def row_sums(b):
        ssrow[b] = jnp.broadcast_to(jnp.sum(ss[b].T, axis=0, keepdims=True), (8, T))

    if groups == 1:
        cin[...] = jnp.zeros_like(cin)
    else:
        @pl.when(group == 0)
        def _():
            cin[...] = jnp.zeros_like(cin)

    def chain(i):
        if groups == 1:
            return

        @pl.when(group > 0)
        def _():
            chain_desc(i, s - 4).wait_recv()

        @pl.when(group < groups - 1)
        def _():
            cout[i] = fold(cin[i], 4, i)
            chain_desc(i, s + 4).start()

    decays(0, ld[...])
    tok_load.wait()
    matmul(0, [d], True)

    sent = [2]

    def tok_next():
        tok_desc(sent[0] - 2).wait_send()
        if sent[0] < N:
            tok_desc(sent[0]).start()
        sent[0] += 1

    def peer_step(k):
        if k == 0:
            ld_copy.wait_recv()
            decays(1, ldp[...])
            tok_desc(0).wait_recv()
            matmul(1, [d], True)
        else:
            first = 2 * k - 1
            for j in range(first, min(first + 2, N)):
                tok_desc(j).wait_recv()
            matmul(1, step_origins(k))

    for k in range(1, K):
        relay(0, k, 0)
        if k > 1:
            collect(0, k - 1)
            matmul(0, step_origins(k - 1))
        relay(0, k, 1)
        tok_next()
        relay(0, k, 2)
        peer_step(k - 1)
        relay(0, k, 3)
        tok_next()
    begin(1)
    relay(0, K, 0)
    relay(0, K, 2)
    collect(0, K - 1)
    matmul(0, step_origins(K - 1))
    relay(0, K, 1)
    relay(0, K, 3)
    tok_next()
    peer_step(K - 1)
    collect(0, K)
    matmul(0, [origin(0, K)])
    head_local(0, 0)
    head_attend(0, 0)
    head_local(0, 1)
    relay(1, 1, 0)
    head_attend(0, 1)
    head_local(0, 2)
    head_attend(0, 2)
    head_local(0, 3)
    relay(1, 1, 1)
    head_attend(0, 3)
    for b in (0, 1):
        tot_desc(b, False).wait_recv()
    for i in range(HX):
        st_desc(0, i, False).wait_recv()
    peer_step(K)
    tok_next()
    head_local(1, 0)
    slots = [(k, p) for k in range(2, K) for p in range(OPIECES)]
    for i in range(HX):
        head_attend(1, i)
        if i + 1 < HX:
            head_local(1, i + 1)
        st_desc(1, i, False).wait_recv()
        chain(i)
        head_final(1, i)
        if i % 2 == 1 and slots:
            relay(1, *slots.pop(0))
    row_sums(1)
    ss_copy.start()
    for i in range(HX):
        head_final(0, i)
    row_sums(0)
    for k, p in slots:
        relay(1, k, p)
    for p in range(OPIECES):
        relay(1, K, p)
    ss_copy.wait_recv()
    inv = lax.rsqrt((ssrow[0, 0:1, :] + ssin[0:1, :]) * (1.0 / F) + 1e-06)
    ss[0] = jnp.broadcast_to(inv, (hd, T)).T
    for i in range(HX):
        g_desc(i, False).wait_recv()
    for k in range(1, K + 1):
        collect(1, k)

    @pl.loop(0, D // tile)
    def _(j):
        cols = pl.ds(pl.multiple_of(j * tile, tile), tile)
        y = jnp.dot(gated[...], WO[:, cols], preferred_element_type=F32)
        scale = jnp.concatenate([ss[0]] * (tile // hd), axis=1)
        out[:, cols] = (y * scale).astype(BF16)

    drain(0)
    drain(1)
    for j in range(sent[0] - 2, N):
        tok_desc(j).wait_send()
    ld_copy.wait_send()
    ss_copy.wait_send()
    for b in (0, 1):
        tot_desc(b, True).wait_send()
        for i in range(HX):
            st_desc(b, i, True).wait_send()
    for i in range(HX):
        g_desc(i, True).wait_send()
    if groups > 1:
        @pl.when(group < groups - 1)
        def _():
            for i in range(HX):
                chain_desc(i, s + 4).wait_send()


def body(n_dp, n_seq, tokens, log_decay, w_qkv, w_gate, w_out, norm_gain):
    tok = tokens[0]
    T, D = tok.shape
    H = log_decay.shape[1]
    F = norm_gain.shape[0]
    hd = F // H
    HX = H // 2
    vm = pl.BlockSpec(memory_space=pltpu.VMEM)
    hbm = pl.BlockSpec(memory_space=pl.ANY)
    dma = pltpu.SemaphoreType.DMA
    V = pltpu.VMEM
    m = n_dp // 2
    y = pl.pallas_call(
        functools.partial(fused, n_dp, n_seq),
        out_shape=jax.ShapeDtypeStruct((T, D), BF16),
        in_specs=[hbm, vm, vm, hbm, hbm, hbm],
        out_specs=vm,
        scratch_shapes=[
            V((T, D), BF16), V((T, D), BF16), V((D, 2 * F), BF16), V((F, D), BF16),
            V((T, 2 * F), F32), V((T, 2 * F), F32),
            V((2, HX, T, hd), BF16), V((2, HX, T, hd), BF16), V((2, HX, T, hd), BF16),
            V((2, HX, T, hd), F32), V((2, HX, T, hd), F32), V((2, HX, 8, T), F32),
            V((2, H, T), F32), V((H, T), F32), V((4, 8, hd), F32), V((4, HX, hd, hd), F32),
            V((HX, hd, hd), F32), V((HX, hd, hd), F32),
            V((2, T, hd), F32), V((2, 8, T), F32), V((8, T), F32), V((T, F), BF16),
            V((HX, T, hd), BF16),
            dma((5,)), dma,
            dma((2, WPIECES, m)), dma((2, WPIECES, m)), dma((2, WPIECES, m)), dma((2, WPIECES, m)),
            dma((2, OPIECES, m)), dma((2, OPIECES, m)), dma((2, OPIECES, m)), dma((2, OPIECES, m)),
            dma((n_dp,)), dma((n_dp,)), dma, dma, dma((2,)), dma((2,)),
            dma((2, HX)), dma((2, HX)), dma((HX,)), dma((HX,)), dma, dma, dma((HX,)), dma((HX,)),
        ],
        compiler_params=pltpu.CompilerParams(
            collective_id=0, has_side_effects=True, vmem_limit_bytes=56 * 1024 * 1024),
    )(tok, log_decay[0], norm_gain[None], w_qkv, w_gate, w_out)
    return y[None]


def solution(mesh):
    placed = (
        P("dp", "seq", None),
        P("dp", None, "seq"),
        P("dp", None),
        P("dp", None),
        P("dp", None),
        P(),
    )
    return jax.shard_map(
        functools.partial(body, mesh.shape["dp"], mesh.shape["seq"]),
        mesh=mesh, in_specs=placed, out_specs=P("dp", "seq", None), check_vma=False
    )
```

```python
import functools

import jax
import jax.numpy as jnp
from jax import lax
from jax.experimental import pallas as pl
from jax.experimental.pallas import tpu as pltpu
from jax.sharding import PartitionSpec as P

MESH = pl.DeviceIdType.MESH
F32 = jnp.float32
BF16 = jnp.bfloat16
PARTS = 4
WPIECES = 4
OPIECES = 4
WINDOW = 3


def fused(n_dp, n_seq, tok_hbm, ld, gain, wqkv, wgate, wout, part, gz, wz, scale,
          tok, tokp, W, WO, acc0, acc1, q_s, k_s, v_s, att, ccol, crow, cums, ldp, tot, st, cin,
          cout, ss, ssrow, ssin, gated, gsend,
          loc_sem, tok_sem, wr, ws, wpr, wps, orr, ors, opr, ops, tr, ts, lr, ls, tor, tos,
          str_, sts, gr, gs, ssr, sss, cr, cs):
    T, D = tok_hbm.shape
    H = ld.shape[0]
    F = gain.shape[1]
    hd = F // H
    HX = H // 2
    FX = F // 2
    N = n_dp
    K = N // 2
    R = D // N
    RO = F // N
    groups = n_seq // 4
    s = lax.axis_index("seq")
    d = lax.axis_index("dp")
    core = s % 2
    x = (s // 2) % 2
    group = s // 4
    partner = s + 1 - 2 * core
    xpeer = s + 2 - 4 * x

    def pos_of(i):
        return jnp.where(i % 2 == 0, i // 2, N - 1 - i // 2)

    def dev_at(p):
        p = lax.rem(p + 2 * N, N)
        return jnp.where(p < K, 2 * p, 2 * (N - 1 - p) + 1)

    pos = pos_of(d)
    ring_to = (dev_at(pos + 1), dev_at(pos - 1))

    def origin(dr, k):
        return dev_at(pos - k) if dr == 0 else dev_at(pos + k)

    def dev(seq=None, dp=None):
        return {"seq": s if seq is None else seq, "dp": d if dp is None else dp}

    def mk(src, dst, ssem, rsem, to):
        return pltpu.make_async_remote_copy(
            src_ref=src, dst_ref=dst, send_sem=ssem, recv_sem=rsem,
            device_id=to, device_id_type=MESH)

    npiece = (WPIECES, OPIECES)
    ring_sems = ((ws, wr, wps, wpr), (ors, orr, ops, opr))

    def piece(ph, dr, k, c, p):
        rows, buf = ((R, W), (RO, WO))[ph]
        width = buf.shape[1] // npiece[ph]
        q = rows // 2
        row = pl.multiple_of(origin(dr, k) * rows + c * q, q)
        return buf.at[pl.ds(row, q), pl.ds(p * width, width)]

    xcol = pl.multiple_of(x * FX, FX)

    def own(ph, p):
        q = (R, RO)[ph] // 2
        rows = pl.ds(pl.multiple_of(core * q, q), q)
        if ph == 1:
            width = D // OPIECES
            return wout.at[rows, pl.ds(p * width, width)]
        if p == 3:
            return wgate.at[rows, pl.ds(xcol, FX)]
        return wqkv.at[rows, pl.ds(p * F + xcol, FX)]

    def has(ph, dr, k, p):
        return k < K or (k == K and (p * 2) // npiece[ph] == dr)

    def ring_desc(ph, dr, k, at, p):
        a, b = ring_sems[ph][:2]
        ref = piece(ph, dr, at, core, p)
        return mk(ref if at else own(ph, p), ref, a.at[dr, p, k - 1], b.at[dr, p, k - 1],
                  dev(dp=ring_to[dr]))

    def part_desc(ph, dr, k, c, p):
        a, b = ring_sems[ph][2:]
        ref = piece(ph, dr, k, c, p)
        return mk(ref, ref, a.at[dr, p, k - 1], b.at[dr, p, k - 1], dev(seq=partner))

    def begin(ph):
        for p in range(npiece[ph]):
            for dr in (0, 1):
                if has(ph, dr, 1, p):
                    ring_desc(ph, dr, 1, 0, p).start()

    def relay(ph, k, p):
        for dr in (0, 1):
            if not has(ph, dr, k, p):
                continue
            ring_desc(ph, dr, k, k, p).wait_recv()
            if has(ph, dr, k + 1, p):
                ring_desc(ph, dr, k + 1, k, p).start()
            part_desc(ph, dr, k, core, p).start()

    def collect(ph, k):
        for dr in (0, 1):
            for p in range(npiece[ph]):
                if has(ph, dr, k, p):
                    part_desc(ph, dr, k, 1 - core, p).wait_recv()

    def drain(ph):
        for k in range(1, K + 1):
            for dr in (0, 1):
                for p in range(npiece[ph]):
                    if has(ph, dr, k, p):
                        ring_desc(ph, dr, k, k, p).wait_send()
                        part_desc(ph, dr, k, core, p).wait_send()

    order = [d] + [origin(dr, k) for k in range(1, K) for dr in (0, 1)] + [origin(0, K)]

    half = T // 2

    def tok_desc(j):
        rows = pl.ds(j // N * half, half)
        cols = pl.ds(pl.multiple_of(order[j % N] * R, R), R)
        return mk(tok_hbm.at[rows, cols], tokp.at[rows, cols], ts.at[j], tr.at[j], dev(seq=xpeer))

    def blk(b):
        return 2 * (x if b == 0 else 1 - x) + core

    def st_desc(b, i, mine):
        ref = st.at[blk(b) if mine else blk(b) + 1 - 2 * core, i]
        return mk(ref, ref, sts.at[b, i], str_.at[b, i], dev(seq=partner))

    def tot_desc(b, mine):
        ref = tot.at[blk(b) if mine else blk(b) + 1 - 2 * core]
        return mk(ref, ref, tos.at[b], tor.at[b], dev(seq=partner))

    def g_desc(i, h, mine):
        c = (x if mine else 1 - x) * FX + i * hd
        rows = pl.ds(h * half, half)
        return mk(gsend.at[i, rows], gated.at[rows, pl.ds(pl.multiple_of(c, hd), hd)],
                  gs.at[h, i], gr.at[h, i], dev(seq=xpeer))

    ld_copy = mk(ld, ldp, ls, lr, dev(seq=xpeer))
    ss_copy = mk(ssrow.at[1], ssin, sss, ssr, dev(seq=xpeer))

    def chain_desc(i, to):
        return mk(cout.at[i], cin.at[i], cs.at[i], cr.at[i], dev(seq=to))

    base = pl.multiple_of(d * R, R)
    loads = []
    for p in range(PARTS):
        src = wgate.at[:, pl.ds(xcol, FX)] if p == 3 else wqkv.at[:, pl.ds(p * F + xcol, FX)]
        loads.append(pltpu.make_async_copy(
            src, W.at[pl.ds(base, R), pl.ds(p * FX, FX)], loc_sem.at[p]))
    loads.append(pltpu.make_async_copy(
        wout, WO.at[pl.ds(pl.multiple_of(d * RO, RO), RO), :], loc_sem.at[4]))
    for c in loads:
        c.start()
    tok_load = pltpu.make_async_copy(tok_hbm, tok, tok_sem)
    tok_load.start()

    barrier = pltpu.get_barrier_semaphore()
    for who in (dev(dp=ring_to[0]), dev(dp=ring_to[1]), dev(seq=partner), dev(seq=xpeer)):
        pl.semaphore_signal(barrier, inc=1, device_id=who, device_id_type=MESH)
    greeted = 4
    if groups > 1:
        @pl.when(group > 0)
        def _():
            pl.semaphore_signal(barrier, inc=1, device_id=dev(seq=s - 4), device_id_type=MESH)

        @pl.when(group < groups - 1)
        def _():
            pl.semaphore_signal(barrier, inc=1, device_id=dev(seq=s + 4), device_id_type=MESH)
        greeted = greeted + jnp.where(group > 0, 1, 0) + jnp.where(group < groups - 1, 1, 0)
    lane = lax.broadcasted_iota(jnp.int32, (H, T), 1)

    def decays(b, rows):
        cum = rows
        step = 1
        while step < T:
            cum = cum + jnp.where(lane >= step, pltpu.roll(cum, step, 1), 0.0)
            step *= 2
        cums[b] = cum
        for i in range(HX):
            row = cums[b, pl.ds(x * HX + i, 1), :]
            crow[b, i] = jnp.broadcast_to(row, (8, T))
            col = jnp.broadcast_to(row, (hd, T)).T
            ccol[b, i] = col
            tot[blk(b), i:i + 1, :] = col[T - 1:T, :]

    toks = (tok, tokp)
    accs = (acc0, acc1)

    def matmul(b, origins, rs=slice(None), first=False):
        rows = [pl.ds(pl.multiple_of(o * R, R), R) for o in origins]
        left = jnp.concatenate([toks[b][rs, r] for r in rows], axis=1)
        right = jnp.concatenate([W[r, :] for r in rows], axis=0)
        y = jnp.dot(left, right, preferred_element_type=F32)
        if first:
            accs[b][rs, :] = y
        else:
            accs[b][rs, :] += y

    def step_origins(k):
        return [origin(0, k)] if k == K else [origin(0, k), origin(1, k)]

    def silu(v):
        return (v / (1.0 + jnp.exp(-v))).astype(BF16)

    halves = (slice(0, half), slice(half, T))

    def head_local(b, i, r=slice(None)):
        a = accs[b]
        k_s[b, i, r, :] = silu(a[r, FX + i * hd:FX + (i + 1) * hd])
        v_s[b, i, r, :] = silu(a[r, 2 * FX + i * hd:2 * FX + (i + 1) * hd])
        q_s[b, i, r, :] = silu(a[r, i * hd:(i + 1) * hd])

    def head_state(b, i):
        c = ccol[b, i]
        sk = (k_s[b, i].astype(F32) * jnp.exp(c[T - 1:T, :] - c)).astype(BF16)
        st[blk(b), i] = lax.dot_general(sk, v_s[b, i], (((0,), (0,)), ((), ())),
                                        preferred_element_type=F32)
        st_desc(b, i, True).start()

    tri = (lax.broadcasted_iota(jnp.int32, (half, half), 1)
           <= lax.broadcasted_iota(jnp.int32, (half, half), 0))

    def head_attend(b, i, u):
        r = halves[u]
        q = q_s[b, i, r, :]
        c = jnp.concatenate([ccol[b, i, r, :]] * (half // hd), axis=1)
        total = None
        for e in range(u + 1):
            z = halves[e]
            sc = lax.dot_general(q, k_s[b, i, z, :], (((1,), (1,)), ((), ())),
                                 preferred_element_type=F32)
            gap = c - crow[b, i, 0:1, z]
            if e == u:
                gap = jnp.where(tri, gap, -1e30)
            w = (sc * jnp.exp(gap)).astype(BF16)
            y = jnp.dot(w, v_s[b, i, z, :], preferred_element_type=F32)
            total = y if total is None else total + y
        att[b, i, r, :] = total

    def fold(first, count, i):
        def one(j, c):
            return jnp.exp(tot[j, i:i + 1, :]) * c + st[j, i]
        return lax.fori_loop(0, count, one, first)

    def head_final(b, i, h):
        r = halves[h]
        carried = fold(cin[i], blk(b), i).astype(BF16)
        inter = jnp.dot(q_s[b, i, r, :], carried, preferred_element_type=F32)
        a = att[b, i, r, :] + inter * jnp.exp(ccol[b, i, r, :])
        if i == 0:
            ss[b, r, :] = a * a
        else:
            ss[b, r, :] += a * a
        g = accs[b][r, 3 * FX + i * hd:3 * FX + (i + 1) * hd]
        f = pl.ds(pl.multiple_of(x * FX + i * hd, hd), hd)
        val = (a * gain[:, f] * (1.0 / (1.0 + jnp.exp(-g)))).astype(BF16)
        if b == 0:
            gated[r, f] = val
        else:
            gsend[i, r, :] = val
            g_desc(i, h, True).start()

    def row_sums(b):
        ssrow[b] = jnp.broadcast_to(jnp.sum(ss[b].T, axis=0, keepdims=True), (8, T))

    if groups == 1:
        cin[...] = jnp.zeros_like(cin)
    else:
        @pl.when(group == 0)
        def _():
            cin[...] = jnp.zeros_like(cin)

    def chain(i):
        if groups == 1:
            return

        @pl.when(group > 0)
        def _():
            chain_desc(i, s - 4).wait_recv()

        @pl.when(group < groups - 1)
        def _():
            cout[i] = fold(cin[i], 4, i)
            chain_desc(i, s + 4).start()

    pl.semaphore_wait(barrier, greeted)
    begin(0)
    started = [0]
    total_toks = 2 * N

    def tok_next():
        j = started[0]
        if j < total_toks:
            if j >= WINDOW:
                tok_desc(j - WINDOW).wait_send()
            tok_desc(j).start()
            started[0] = j + 1

    def tok_need(j):
        while started[0] <= min(j + WINDOW - 1, total_toks - 1):
            tok_next()
        tok_desc(j).wait_recv()

    for _ in range(WINDOW):
        tok_next()
    ld_copy.start()
    decays(0, ld[...])
    tot_desc(0, True).start()
    for c in loads:
        c.wait()
    tok_load.wait()
    matmul(0, [d], first=True)

    def peer_step(h, k):
        for j in ([0] if k == 0 else range(2 * k - 1, min(2 * k + 1, N))):
            tok_need(h * N + j)
        matmul(1, [d] if k == 0 else step_origins(k), halves[h], k == 0)

    late = [0]
    wo = ([(k, p) for k in range(1, K) for p in range(OPIECES)]
          + [(K, p) for a in range(OPIECES // 2) for p in (a, a + OPIECES // 2)])

    def wo_next(n=1):
        for _ in range(n):
            if wo:
                k, p = wo.pop(0)
                relay(1, k, p)
                if k == K:
                    relay(1, *wo.pop(0))

    for k in range(1, K):
        relay(0, k, 0)
        tok_next()
        if k > 1:
            collect(0, k - 1)
            matmul(0, step_origins(k - 1))
        relay(0, k, 1)
        tok_next()
        if k == 1:
            ld_copy.wait_recv()
            decays(1, ldp[...])
            tot_desc(1, True).start()
        peer_step(0, k - 1)
        relay(0, k, 2)
        tok_next()
        relay(0, k, 3)
        tok_next()
        while N + 2 * late[0] <= 4 * k - 2:
            peer_step(1, late[0])
            late[0] += 1
    begin(1)
    relay(0, K, 0)
    relay(0, K, 2)
    tok_next()
    collect(0, K - 1)
    matmul(0, step_origins(K - 1))
    peer_step(0, K - 1)
    relay(0, K, 1)
    relay(0, K, 3)
    tok_next()
    while late[0] < K - 1:
        peer_step(1, late[0])
        late[0] += 1
    collect(0, K)
    matmul(0, step_origins(K))
    peer_step(0, K)
    for i in range(HX):
        head_local(0, i)
        head_state(0, i)
    for b in (0, 1):
        tot_desc(b, False).wait_recv()
    wo_next()
    for i in range(HX):
        head_local(1, i, halves[0])
        head_attend(1, i, 0)
    wo_next()
    for i in range(HX):
        st_desc(0, i, False).wait_recv()
    early = groups == 1
    if early:
        @pl.when(core == 0)
        def _():
            for i in range(HX):
                head_final(1, i, 0)
    wo_next()
    while late[0] <= K:
        peer_step(1, late[0])
        late[0] += 1
    wo_next()
    for i in range(HX):
        head_local(1, i, halves[1])
        head_state(1, i)
    wo_next()
    head_attend(1, 0, 1)
    for i in range(HX):
        st_desc(1, i, False).wait_recv()
        chain(i)
    if early:
        @pl.when(core == 1)
        def _():
            for i in range(HX):
                head_final(1, i, 0)
    else:
        for i in range(HX):
            head_final(1, i, 0)
    wo_next()
    for i in range(HX):
        if i:
            head_attend(1, i, 1)
        head_final(1, i, 1)
    row_sums(1)
    ss_copy.start()
    wo_next()
    for i in range(HX):
        for h in (0, 1):
            head_attend(0, i, h)
            head_final(0, i, h)
        if i % 2 == 1:
            wo_next()
    row_sums(0)
    while wo and wo[0][0] < K:
        wo_next()
    for k in range(1, K):
        collect(1, k)
    ss_copy.wait_recv()
    inv = lax.rsqrt((ssrow[0, 0:1, :] + ssin[0:1, :]) * (1.0 / F) + 1e-06)
    ss[0] = jnp.broadcast_to(inv, (hd, T)).T
    for i in range(HX):
        for h in (0, 1):
            g_desc(i, h, False).wait_recv()

    split = RO % 128 == 0
    last = order[-1:] if split else []
    done = order[:-1] if split else []

    def mix(origins, cols):
        at = [pl.ds(pl.multiple_of(o * RO, RO), RO) for o in origins]
        left = jnp.concatenate([gated[:, r] for r in at], axis=1)
        right = jnp.concatenate([WO[r, cols] for r in at], axis=0)
        return jnp.dot(left, right, preferred_element_type=F32)

    for u in range(4):
        cols = slice(u * D // 4, (u + 1) * D // 4)
        if split:
            part[:, cols] = mix(done, cols)
        if u in (0, 2):
            wo_next()
    while wo:
        wo_next()
    scale[...] = ss[0]
    collect(1, K)
    if split:
        gz[...] = gated[:, pl.ds(pl.multiple_of(last[0] * RO, RO), RO)]
        wz[...] = WO[pl.ds(pl.multiple_of(last[0] * RO, RO), RO), :]
    else:
        part[...] = jnp.dot(gated[...], WO[...], preferred_element_type=F32)
        gz[...] = jnp.zeros_like(gz)
        wz[...] = jnp.zeros_like(wz)

    drain(0)
    drain(1)
    for j in range(total_toks - WINDOW, total_toks):
        tok_desc(j).wait_send()
    ld_copy.wait_send()
    ss_copy.wait_send()
    for b in (0, 1):
        tot_desc(b, True).wait_send()
        for i in range(HX):
            st_desc(b, i, True).wait_send()
    for i in range(HX):
        for h in (0, 1):
            g_desc(i, h, True).wait_send()
    if groups > 1:
        @pl.when(group < groups - 1)
        def _():
            for i in range(HX):
                chain_desc(i, s + 4).wait_send()


def finish(part, gz, wz, scale, out, ob, sem):
    D = part.shape[1]
    width = D // 4
    copies = []
    for u in range(4):
        cols = slice(u * width, (u + 1) * width)
        y = part[:, cols] + jnp.dot(gz[...], wz[:, cols], preferred_element_type=F32)
        wide = jnp.concatenate([scale[...]] * (width // scale.shape[1]), axis=1)
        ob[:, cols] = (y * wide).astype(BF16)
        c = pltpu.make_async_copy(ob.at[:, cols], out.at[:, cols], sem.at[u])
        c.start()
        copies.append(c)
    for c in copies:
        c.wait()


def body(n_dp, n_seq, tokens, log_decay, w_qkv, w_gate, w_out, norm_gain):
    tok = tokens[0]
    T, D = tok.shape
    H = log_decay.shape[1]
    F = norm_gain.shape[0]
    hd = F // H
    HX = H // 2
    vm = pl.BlockSpec(memory_space=pltpu.VMEM)
    hbm = pl.BlockSpec(memory_space=pl.ANY)
    dma = pltpu.SemaphoreType.DMA
    V = pltpu.VMEM
    m = n_dp // 2
    RO = F // n_dp
    parts = pl.pallas_call(
        functools.partial(fused, n_dp, n_seq),
        out_shape=(V((T, D), F32), V((T, RO), BF16), V((RO, D), BF16), V((T, hd), F32)),
        in_specs=[hbm, vm, vm, hbm, hbm, hbm],
        out_specs=(vm, vm, vm, vm),
        scratch_shapes=[
            V((T, D), BF16), V((T, D), BF16), V((D, 2 * F), BF16), V((F, D), BF16),
            V((T, 2 * F), F32), V((T, 2 * F), F32),
            V((2, HX, T, hd), BF16), V((2, HX, T, hd), BF16), V((2, HX, T, hd), BF16),
            V((2, HX, T, hd), F32), V((2, HX, T, hd), F32), V((2, HX, 8, T), F32),
            V((2, H, T), F32), V((H, T), F32), V((4, 8, hd), F32), V((4, HX, hd, hd), F32),
            V((HX, hd, hd), F32), V((HX, hd, hd), F32),
            V((2, T, hd), F32), V((2, 8, T), F32), V((8, T), F32), V((T, F), BF16),
            V((HX, T, hd), BF16),
            dma((5,)), dma,
            dma((2, WPIECES, m)), dma((2, WPIECES, m)), dma((2, WPIECES, m)), dma((2, WPIECES, m)),
            dma((2, OPIECES, m)), dma((2, OPIECES, m)), dma((2, OPIECES, m)), dma((2, OPIECES, m)),
            dma((2 * n_dp,)), dma((2 * n_dp,)), dma, dma, dma((2,)), dma((2,)),
            dma((2, HX)), dma((2, HX)), dma((2, HX)), dma((2, HX)), dma, dma, dma((HX,)), dma((HX,)),
        ],
        compiler_params=pltpu.CompilerParams(
            collective_id=0, has_side_effects=True, vmem_limit_bytes=57 * 1024 * 1024),
    )(tok, log_decay[0], norm_gain[None], w_qkv, w_gate, w_out)
    y = pl.pallas_call(
        finish,
        out_shape=jax.ShapeDtypeStruct((T, D), BF16),
        in_specs=[vm] * 4,
        out_specs=hbm,
        scratch_shapes=[V((T, D), BF16), dma((4,))],
        compiler_params=pltpu.CompilerParams(vmem_limit_bytes=8 * 1024 * 1024),
    )(*[pltpu.with_memory_space_constraint(a, pltpu.VMEM) for a in parts])
    return y[None]


def solution(mesh):
    placed = (
        P("dp", "seq", None),
        P("dp", None, "seq"),
        P("dp", None),
        P("dp", None),
        P("dp", None),
        P(),
    )
    return jax.shard_map(
        functools.partial(body, mesh.shape["dp"], mesh.shape["seq"]),
        mesh=mesh, in_specs=placed, out_specs=P("dp", "seq", None), check_vma=False
    )
```

```python
import functools

import jax
import jax.numpy as jnp
from jax import lax
from jax.experimental import pallas as pl
from jax.experimental.pallas import tpu as pltpu
from jax.sharding import PartitionSpec as P

MESH = pl.DeviceIdType.MESH
F32 = jnp.float32
BF16 = jnp.bfloat16
PARTS = 4
WPIECES = 4
OPIECES = 4
WINDOW = 3
PLAN = "CEFHJKMOQ"


def fused(n_dp, n_seq, tok_hbm, ld_hbm, gain_hbm, wqkv, wgate, wout, part, gz, wz, scale,
          tok, tokp, ld, gain, W, WO, acc0, acc1, q_s, k_s, v_s, att, ccol, crow, cums, ldp, tot, st, cin,
          cout, ss, ssrow, ssin, gated, gsend, car,
          loc_sem, tok_sem, wr, ws, wpr, wps, orr, ors, opr, ops, tr, ts, lr, ls, tor, tos,
          str_, sts, gr, gs, ssr, sss, cr, cs):
    T, D = tok_hbm.shape
    H = ld_hbm.shape[0]
    F = gain_hbm.shape[1]
    hd = F // H
    HX = H // 2
    FX = F // 2
    N = n_dp
    K = N // 2
    R = D // N
    RO = F // N
    groups = n_seq // 4
    s = lax.axis_index("seq")
    d = lax.axis_index("dp")
    core = s % 2
    x = (s // 2) % 2
    group = s // 4
    partner = s + 1 - 2 * core
    xpeer = s + 2 - 4 * x

    def pos_of(i):
        return jnp.where(i % 2 == 0, i // 2, N - 1 - i // 2)

    def dev_at(p):
        p = lax.rem(p + 2 * N, N)
        return jnp.where(p < K, 2 * p, 2 * (N - 1 - p) + 1)

    pos = pos_of(d)
    ring_to = (dev_at(pos + 1), dev_at(pos - 1))

    def origin(dr, k):
        return dev_at(pos - k) if dr == 0 else dev_at(pos + k)

    def dev(seq=None, dp=None):
        return {"seq": s if seq is None else seq, "dp": d if dp is None else dp}

    def mk(src, dst, ssem, rsem, to):
        return pltpu.make_async_remote_copy(
            src_ref=src, dst_ref=dst, send_sem=ssem, recv_sem=rsem,
            device_id=to, device_id_type=MESH)

    npiece = (WPIECES, OPIECES)
    ring_sems = ((ws, wr, wps, wpr), (ors, orr, ops, opr))

    def piece(ph, dr, k, c, p):
        rows, buf = ((R, W), (RO, WO))[ph]
        width = buf.shape[1] // npiece[ph]
        q = rows // 2
        row = pl.multiple_of(origin(dr, k) * rows + c * q, q)
        return buf.at[pl.ds(row, q), pl.ds(p * width, width)]

    xcol = pl.multiple_of(x * FX, FX)

    def own(ph, p):
        q = (R, RO)[ph] // 2
        rows = pl.ds(pl.multiple_of(core * q, q), q)
        if ph == 1:
            width = D // OPIECES
            return wout.at[rows, pl.ds(p * width, width)]
        if p == 3:
            return wgate.at[rows, pl.ds(xcol, FX)]
        return wqkv.at[rows, pl.ds(p * F + xcol, FX)]

    def has(ph, dr, k, p):
        return k < K or (k == K and (p * 2) // npiece[ph] == dr)

    def ring_desc(ph, dr, k, at, p):
        a, b = ring_sems[ph][:2]
        ref = piece(ph, dr, at, core, p)
        return mk(ref if at else own(ph, p), ref, a.at[dr, p, k - 1], b.at[dr, p, k - 1],
                  dev(dp=ring_to[dr]))

    def part_desc(ph, dr, k, c, p):
        a, b = ring_sems[ph][2:]
        ref = piece(ph, dr, k, c, p)
        return mk(ref, ref, a.at[dr, p, k - 1], b.at[dr, p, k - 1], dev(seq=partner))

    def begin(ph):
        for p in range(npiece[ph]):
            for dr in (0, 1):
                if has(ph, dr, 1, p):
                    ring_desc(ph, dr, 1, 0, p).start()

    def relay(ph, k, p):
        for dr in (0, 1):
            if not has(ph, dr, k, p):
                continue
            ring_desc(ph, dr, k, k, p).wait_recv()
            if has(ph, dr, k + 1, p):
                ring_desc(ph, dr, k + 1, k, p).start()
            part_desc(ph, dr, k, core, p).start()

    def collect(ph, k):
        for dr in (0, 1):
            for p in range(npiece[ph]):
                if has(ph, dr, k, p):
                    part_desc(ph, dr, k, 1 - core, p).wait_recv()

    def drain(ph, ks):
        for k in ks:
            for dr in (0, 1):
                for p in range(npiece[ph]):
                    if has(ph, dr, k, p):
                        ring_desc(ph, dr, k, k, p).wait_send()
                        part_desc(ph, dr, k, core, p).wait_send()

    order = [d] + [origin(dr, k) for k in range(1, K) for dr in (0, 1)] + [origin(0, K)]

    half = T // 2

    def tok_desc(j):
        rows = pl.ds(j // N * half, half)
        cols = pl.ds(pl.multiple_of(order[j % N] * R, R), R)
        return mk(tok_hbm.at[rows, cols], tokp.at[rows, cols], ts.at[j], tr.at[j], dev(seq=xpeer))

    def blk(b):
        return 2 * (x if b == 0 else 1 - x) + core

    def st_desc(b, i, mine):
        ref = st.at[blk(b) if mine else blk(b) + 1 - 2 * core, i]
        return mk(ref, ref, sts.at[b, i], str_.at[b, i], dev(seq=partner))

    def tot_desc(b, mine):
        ref = tot.at[blk(b) if mine else blk(b) + 1 - 2 * core]
        return mk(ref, ref, tos.at[b], tor.at[b], dev(seq=partner))

    def g_desc(i, h, mine):
        c = (x if mine else 1 - x) * FX + i * hd
        rows = pl.ds(h * half, half)
        return mk(gsend.at[i, rows], gated.at[rows, pl.ds(pl.multiple_of(c, hd), hd)],
                  gs.at[h, i], gr.at[h, i], dev(seq=xpeer))

    ld_copy = mk(ld_hbm, ldp, ls, lr, dev(seq=xpeer))
    ss_copy = mk(ssrow.at[1], ssin, sss, ssr, dev(seq=xpeer))

    def chain_desc(i, to):
        return mk(cout.at[i], cin.at[i], cs.at[i], cr.at[i], dev(seq=to))

    barrier = pltpu.get_barrier_semaphore()
    for who in (dev(dp=ring_to[0]), dev(dp=ring_to[1]), dev(seq=partner), dev(seq=xpeer)):
        pl.semaphore_signal(barrier, inc=1, device_id=who, device_id_type=MESH)
    greeted = 4
    if groups > 1:
        @pl.when(group > 0)
        def _():
            pl.semaphore_signal(barrier, inc=1, device_id=dev(seq=s - 4), device_id_type=MESH)

        @pl.when(group < groups - 1)
        def _():
            pl.semaphore_signal(barrier, inc=1, device_id=dev(seq=s + 4), device_id_type=MESH)
        greeted = greeted + jnp.where(group > 0, 1, 0) + jnp.where(group < groups - 1, 1, 0)
    base = pl.multiple_of(d * R, R)
    loads = []
    for p in range(PARTS):
        src = wgate.at[:, pl.ds(xcol, FX)] if p == 3 else wqkv.at[:, pl.ds(p * F + xcol, FX)]
        loads.append(pltpu.make_async_copy(
            src, W.at[pl.ds(base, R), pl.ds(p * FX, FX)], loc_sem.at[p]))
    loads.append(pltpu.make_async_copy(
        wout, WO.at[pl.ds(pl.multiple_of(d * RO, RO), RO), :], loc_sem.at[4]))
    for c in loads:
        c.start()
    tok_load = pltpu.make_async_copy(tok_hbm, tok, tok_sem)
    tok_load.start()
    small = [pltpu.make_async_copy(ld_hbm, ld, loc_sem.at[5]),
             pltpu.make_async_copy(gain_hbm, gain, loc_sem.at[6])]
    for c in small:
        c.start()

    lane = lax.broadcasted_iota(jnp.int32, (H, T), 1)

    def decays(b, rows):
        cum = rows
        step = 1
        while step < T:
            cum = cum + jnp.where(lane >= step, pltpu.roll(cum, step, 1), 0.0)
            step *= 2
        cums[b] = cum
        for i in range(HX):
            row = cums[b, pl.ds(x * HX + i, 1), :]
            crow[b, i] = jnp.broadcast_to(row, (8, T))
            col = jnp.broadcast_to(row, (hd, T)).T
            ccol[b, i] = col
            tot[blk(b), i:i + 1, :] = col[T - 1:T, :]

    toks = (tok, tokp)
    accs = (acc0, acc1)

    def matmul(b, origins, rs=slice(None), first=False):
        rows = [pl.ds(pl.multiple_of(o * R, R), R) for o in origins]
        left = jnp.concatenate([toks[b][rs, r] for r in rows], axis=1)
        right = jnp.concatenate([W[r, :] for r in rows], axis=0)
        y = jnp.dot(left, right, preferred_element_type=F32)
        if first:
            accs[b][rs, :] = y
        else:
            accs[b][rs, :] += y

    def step_origins(k):
        return [origin(0, k)] if k == K else [origin(0, k), origin(1, k)]

    def silu(v):
        return (v / (1.0 + jnp.exp(-v))).astype(BF16)

    halves = (slice(0, half), slice(half, T))

    def head_local(b, i, r=slice(None)):
        a = accs[b]
        k_s[b, i, r, :] = silu(a[r, FX + i * hd:FX + (i + 1) * hd])
        v_s[b, i, r, :] = silu(a[r, 2 * FX + i * hd:2 * FX + (i + 1) * hd])
        q_s[b, i, r, :] = silu(a[r, i * hd:(i + 1) * hd])

    def head_state(b, i):
        c = ccol[b, i]
        sk = (k_s[b, i].astype(F32) * jnp.exp(c[T - 1:T, :] - c)).astype(BF16)
        st[blk(b), i] = lax.dot_general(sk, v_s[b, i], (((0,), (0,)), ((), ())),
                                        preferred_element_type=F32)
        st_desc(b, i, True).start()

    tri = (lax.broadcasted_iota(jnp.int32, (half, half), 1)
           <= lax.broadcasted_iota(jnp.int32, (half, half), 0))

    def head_attend(b, i, u):
        r = halves[u]
        q = q_s[b, i, r, :]
        c = jnp.concatenate([ccol[b, i, r, :]] * (half // hd), axis=1)
        total = None
        for e in range(u + 1):
            z = halves[e]
            sc = lax.dot_general(q, k_s[b, i, z, :], (((1,), (1,)), ((), ())),
                                 preferred_element_type=F32)
            gap = c - crow[b, i, 0:1, z]
            if e == u:
                gap = jnp.where(tri, gap, -1e30)
            w = (sc * jnp.exp(gap)).astype(BF16)
            y = jnp.dot(w, v_s[b, i, z, :], preferred_element_type=F32)
            total = y if total is None else total + y
        att[b, i, r, :] = total

    def fold(first, count, i):
        def one(j, c):
            return jnp.exp(tot[j, i:i + 1, :]) * c + st[j, i]
        return lax.fori_loop(0, count, one, first)

    def head_final(b, i, h):
        r = halves[h]
        if h == 0:
            car[b, i] = fold(cin[i], blk(b), i).astype(BF16)
        inter = jnp.dot(q_s[b, i, r, :], car[b, i], preferred_element_type=F32)
        a = att[b, i, r, :] + inter * jnp.exp(ccol[b, i, r, :])
        if i == 0:
            ss[b, r, :] = a * a
        else:
            ss[b, r, :] += a * a
        g = accs[b][r, 3 * FX + i * hd:3 * FX + (i + 1) * hd]
        f = pl.ds(pl.multiple_of(x * FX + i * hd, hd), hd)
        val = (a * gain[:, f] * (1.0 / (1.0 + jnp.exp(-g)))).astype(BF16)
        if b == 0:
            gated[r, f] = val
        else:
            gsend[i, r, :] = val
            g_desc(i, h, True).start()

    def row_sums(b):
        ssrow[b] = jnp.broadcast_to(jnp.sum(ss[b].T, axis=0, keepdims=True), (8, T))

    if groups == 1:
        cin[...] = jnp.zeros_like(cin)
    else:
        @pl.when(group == 0)
        def _():
            cin[...] = jnp.zeros_like(cin)

    def chain(i):
        if groups == 1:
            return

        @pl.when(group > 0)
        def _():
            chain_desc(i, s - 4).wait_recv()

        @pl.when(group < groups - 1)
        def _():
            cout[i] = fold(cin[i], 4, i)
            chain_desc(i, s + 4).start()

    pl.semaphore_wait(barrier, greeted)
    begin(0)
    started = [0]
    total_toks = 2 * N

    def tok_next():
        j = started[0]
        if j < total_toks:
            if j >= WINDOW:
                tok_desc(j - WINDOW).wait_send()
            tok_desc(j).start()
            started[0] = j + 1

    def tok_need(j):
        while started[0] <= min(j + WINDOW - 1, total_toks - 1):
            tok_next()
        tok_desc(j).wait_recv()

    for _ in range(WINDOW):
        tok_next()
    ld_copy.start()
    for c in small:
        c.wait()
    decays(0, ld[...])
    tot_desc(0, True).start()
    for c in loads:
        c.wait()
    tok_load.wait()
    matmul(0, [d], first=True)

    def peer_step(h, k):
        for j in ([0] if k == 0 else range(2 * k - 1, min(2 * k + 1, N))):
            tok_need(h * N + j)
        matmul(1, [d] if k == 0 else step_origins(k), halves[h], k == 0)

    late = [0]
    wo = ([(k, p) for k in range(1, K) for p in range(OPIECES)]
          + [(K, p) for a in range(OPIECES // 2) for p in (a, a + OPIECES // 2)])

    def wo_next(n=1):
        for _ in range(n):
            if wo:
                k, p = wo.pop(0)
                relay(1, k, p)
                if k == K:
                    relay(1, *wo.pop(0))

    for k in range(1, K):
        relay(0, k, 0)
        tok_next()
        if k > 1:
            collect(0, k - 1)
            matmul(0, step_origins(k - 1))
        relay(0, k, 1)
        tok_next()
        if k == 1:
            ld_copy.wait_recv()
            decays(1, ldp[...])
            tot_desc(1, True).start()
        peer_step(0, k - 1)
        relay(0, k, 2)
        tok_next()
        relay(0, k, 3)
        tok_next()
        while N + 2 * late[0] <= 4 * k - 2:
            peer_step(1, late[0])
            late[0] += 1
    begin(1)
    relay(0, K, 0)
    relay(0, K, 2)
    tok_next()
    collect(0, K - 1)
    matmul(0, step_origins(K - 1))
    peer_step(0, K - 1)
    relay(0, K, 1)
    relay(0, K, 3)
    tok_next()
    while late[0] < K - 1:
        peer_step(1, late[0])
        late[0] += 1
    collect(0, K)
    matmul(0, step_origins(K))
    peer_step(0, K)
    def relay_at(point):
        wo_next(PLAN.count(point))

    for i in range(HX):
        head_local(0, i)
        head_state(0, i)
        if i == 1:
            relay_at("B")
    for b in (0, 1):
        tot_desc(b, False).wait_recv()
    relay_at("C")
    for i in range(HX):
        head_local(1, i, halves[0])
        head_attend(1, i, 0)
        if i == 1:
            relay_at("D")
    relay_at("E")
    for i in range(HX):
        st_desc(0, i, False).wait_recv()
    early = groups == 1
    if early:
        @pl.when(core == 0)
        def _():
            for i in range(HX):
                head_final(1, i, 0)
    relay_at("F")
    while late[0] <= K:
        peer_step(1, late[0])
        late[0] += 1
        relay_at("G" if late[0] <= K else "H")
    for i in range(HX):
        head_local(1, i, halves[1])
        head_state(1, i)
        if i == 1:
            relay_at("I")
    relay_at("J")
    head_attend(1, 0, 1)
    for i in range(HX):
        st_desc(1, i, False).wait_recv()
        chain(i)
    if early:
        @pl.when(core == 1)
        def _():
            for i in range(HX):
                head_final(1, i, 0)
    else:
        for i in range(HX):
            head_final(1, i, 0)
    relay_at("K")
    for i in range(HX):
        if i:
            head_attend(1, i, 1)
        head_final(1, i, 1)
        if i == 1:
            relay_at("L")
    row_sums(1)
    ss_copy.start()
    relay_at("M")
    for i in range(HX):
        for h in (0, 1):
            head_attend(0, i, h)
            head_final(0, i, h)
        relay_at("NOPQ"[i % 4])
    row_sums(0)
    while wo and wo[0][0] < K:
        wo_next()
    for k in range(1, K):
        collect(1, k)
    drain(0, range(1, K + 1))
    for j in range(total_toks - WINDOW, total_toks):
        tok_desc(j).wait_send()
    ld_copy.wait_send()
    for b in (0, 1):
        tot_desc(b, True).wait_send()
        for i in range(HX):
            st_desc(b, i, True).wait_send()
    ss_copy.wait_recv()
    inv = lax.rsqrt((ssrow[0, 0:1, :] + ssin[0:1, :]) * (1.0 / F) + 1e-06)
    ss[0] = jnp.broadcast_to(inv, (hd, T)).T
    for i in range(HX):
        for h in (0, 1):
            g_desc(i, h, False).wait_recv()

    split = RO % 128 == 0
    last = order[-1:] if split else []
    done = order[:-1] if split else []

    def mix(origins, cols):
        at = [pl.ds(pl.multiple_of(o * RO, RO), RO) for o in origins]
        left = jnp.concatenate([gated[:, r] for r in at], axis=1)
        right = jnp.concatenate([WO[r, cols] for r in at], axis=0)
        return jnp.dot(left, right, preferred_element_type=F32)

    for u in range(4):
        cols = slice(u * D // 4, (u + 1) * D // 4)
        if split:
            part[:, cols] = mix(done, cols)
        if u in (0, 2):
            wo_next()
    while wo:
        wo_next()
    scale[...] = ss[0]
    drain(1, range(1, K))
    collect(1, K)
    if split:
        gz[...] = gated[:, pl.ds(pl.multiple_of(last[0] * RO, RO), RO)]
        wz[...] = WO[pl.ds(pl.multiple_of(last[0] * RO, RO), RO), :]
    else:
        part[...] = jnp.dot(gated[...], WO[...], preferred_element_type=F32)
        gz[...] = jnp.zeros_like(gz)
        wz[...] = jnp.zeros_like(wz)

    drain(1, range(K, K + 1))
    for i in range(HX):
        for h in (0, 1):
            g_desc(i, h, True).wait_send()
    ss_copy.wait_send()
    if groups > 1:
        @pl.when(group < groups - 1)
        def _():
            for i in range(HX):
                chain_desc(i, s + 4).wait_send()


def finish(part, gz, wz, scale, out, ob, sem):
    D = part.shape[1]
    width = D // 4
    copies = []
    for u in range(4):
        cols = slice(u * width, (u + 1) * width)
        y = part[:, cols] + jnp.dot(gz[...], wz[:, cols], preferred_element_type=F32)
        wide = jnp.concatenate([scale[...]] * (width // scale.shape[1]), axis=1)
        ob[:, cols] = (y * wide).astype(BF16)
        c = pltpu.make_async_copy(ob.at[:, cols], out.at[:, cols], sem.at[u])
        c.start()
        copies.append(c)
    for c in copies:
        c.wait()


def body(n_dp, n_seq, tokens, log_decay, w_qkv, w_gate, w_out, norm_gain):
    tok = tokens[0]
    T, D = tok.shape
    H = log_decay.shape[1]
    F = norm_gain.shape[0]
    hd = F // H
    HX = H // 2
    vm = pl.BlockSpec(memory_space=pltpu.VMEM)
    hbm = pl.BlockSpec(memory_space=pl.ANY)
    dma = pltpu.SemaphoreType.DMA
    V = pltpu.VMEM
    m = n_dp // 2
    RO = F // n_dp
    parts = pl.pallas_call(
        functools.partial(fused, n_dp, n_seq),
        out_shape=(V((T, D), F32), V((T, RO), BF16), V((RO, D), BF16), V((T, hd), F32)),
        in_specs=[hbm] * 6,
        out_specs=(vm, vm, vm, vm),
        scratch_shapes=[
            V((T, D), BF16), V((T, D), BF16), V((H, T), F32), V((1, F), F32), V((D, 2 * F), BF16), V((F, D), BF16),
            V((T, 2 * F), F32), V((T, 2 * F), F32),
            V((2, HX, T, hd), BF16), V((2, HX, T, hd), BF16), V((2, HX, T, hd), BF16),
            V((2, HX, T, hd), F32), V((2, HX, T, hd), F32), V((2, HX, 8, T), F32),
            V((2, H, T), F32), V((H, T), F32), V((4, 8, hd), F32), V((4, HX, hd, hd), F32),
            V((HX, hd, hd), F32), V((HX, hd, hd), F32),
            V((2, T, hd), F32), V((2, 8, T), F32), V((8, T), F32), V((T, F), BF16),
            V((HX, T, hd), BF16), V((2, HX, hd, hd), BF16),
            dma((7,)), dma,
            dma((2, WPIECES, m)), dma((2, WPIECES, m)), dma((2, WPIECES, m)), dma((2, WPIECES, m)),
            dma((2, OPIECES, m)), dma((2, OPIECES, m)), dma((2, OPIECES, m)), dma((2, OPIECES, m)),
            dma((2 * n_dp,)), dma((2 * n_dp,)), dma, dma, dma((2,)), dma((2,)),
            dma((2, HX)), dma((2, HX)), dma((2, HX)), dma((2, HX)), dma, dma, dma((HX,)), dma((HX,)),
        ],
        compiler_params=pltpu.CompilerParams(
            collective_id=0, has_side_effects=True, vmem_limit_bytes=57 * 1024 * 1024),
    )(tok, log_decay[0], norm_gain[None], w_qkv, w_gate, w_out)
    y = pl.pallas_call(
        finish,
        out_shape=jax.ShapeDtypeStruct((T, D), BF16),
        in_specs=[vm] * 4,
        out_specs=hbm,
        scratch_shapes=[V((T, D), BF16), dma((4,))],
        compiler_params=pltpu.CompilerParams(vmem_limit_bytes=8 * 1024 * 1024),
    )(*[pltpu.with_memory_space_constraint(a, pltpu.VMEM) for a in parts])
    return y[None]


def solution(mesh):
    placed = (
        P("dp", "seq", None),
        P("dp", None, "seq"),
        P("dp", None),
        P("dp", None),
        P("dp", None),
        P(),
    )
    return jax.shard_map(
        functools.partial(body, mesh.shape["dp"], mesh.shape["seq"]),
        mesh=mesh, in_specs=placed, out_specs=P("dp", "seq", None), check_vma=False
    )
```

```python
import functools

import jax
import jax.numpy as jnp
from jax import lax
from jax.experimental import pallas as pl
from jax.experimental.pallas import tpu as pltpu
from jax.sharding import PartitionSpec as P

MESH = pl.DeviceIdType.MESH
F32 = jnp.float32
BF16 = jnp.bfloat16
PARTS = 4
WPIECES = 4
OPIECES = 4
WINDOW = 3
PLAN = "CEFHJKMOQ"


def fused(n_dp, n_seq, tok_hbm, ld_hbm, gain_hbm, wqkv, wgate, wout, part, gz, wz, scale,
          tok, tokp, ld, gain, W, WO, acc0, acc1, q_s, k_s, v_s, att, ccol, crow, cums, ldp, tot, st, cin,
          cout, ss, ssrow, ssin, gated, gsend, car,
          loc_sem, tok_sem, wr, ws, wpr, wps, orr, ors, opr, ops, tr, ts, lr, ls, tor, tos,
          str_, sts, gr, gs, ssr, sss, cr, cs):
    T, D = tok_hbm.shape
    H = ld_hbm.shape[0]
    F = gain_hbm.shape[1]
    hd = F // H
    HX = H // 2
    FX = F // 2
    N = n_dp
    K = N // 2
    R = D // N
    RO = F // N
    groups = n_seq // 4
    s = lax.axis_index("seq")
    d = lax.axis_index("dp")
    core = s % 2
    x = (s // 2) % 2
    group = s // 4
    partner = s + 1 - 2 * core
    xpeer = s + 2 - 4 * x

    def pos_of(i):
        return jnp.where(i % 2 == 0, i // 2, N - 1 - i // 2)

    def dev_at(p):
        p = lax.rem(p + 2 * N, N)
        return jnp.where(p < K, 2 * p, 2 * (N - 1 - p) + 1)

    pos = pos_of(d)
    ring_to = (dev_at(pos + 1), dev_at(pos - 1))

    def origin(dr, k):
        return dev_at(pos - k) if dr == 0 else dev_at(pos + k)

    def dev(seq=None, dp=None):
        return {"seq": s if seq is None else seq, "dp": d if dp is None else dp}

    def mk(src, dst, ssem, rsem, to):
        return pltpu.make_async_remote_copy(
            src_ref=src, dst_ref=dst, send_sem=ssem, recv_sem=rsem,
            device_id=to, device_id_type=MESH)

    npiece = (WPIECES, OPIECES)
    ring_sems = ((ws, wr, wps, wpr), (ors, orr, ops, opr))

    def piece(ph, dr, k, c, p):
        rows, buf = ((R, W), (RO, WO))[ph]
        width = buf.shape[1] // npiece[ph]
        q = rows // 2
        row = pl.multiple_of(origin(dr, k) * rows + c * q, q)
        return buf.at[pl.ds(row, q), pl.ds(p * width, width)]

    xcol = pl.multiple_of(x * FX, FX)

    def own(ph, p):
        q = (R, RO)[ph] // 2
        rows = pl.ds(pl.multiple_of(core * q, q), q)
        if ph == 1:
            width = D // OPIECES
            return wout.at[rows, pl.ds(p * width, width)]
        if p == 3:
            return wgate.at[rows, pl.ds(xcol, FX)]
        return wqkv.at[rows, pl.ds(p * F + xcol, FX)]

    def has(ph, dr, k, p):
        return k < K or (k == K and (p * 2) // npiece[ph] == dr)

    def ring_desc(ph, dr, k, at, p):
        a, b = ring_sems[ph][:2]
        ref = piece(ph, dr, at, core, p)
        return mk(ref if at else own(ph, p), ref, a.at[dr, p, k - 1], b.at[dr, p, k - 1],
                  dev(dp=ring_to[dr]))

    def part_desc(ph, dr, k, c, p):
        a, b = ring_sems[ph][2:]
        ref = piece(ph, dr, k, c, p)
        return mk(ref, ref, a.at[dr, p, k - 1], b.at[dr, p, k - 1], dev(seq=partner))

    def begin(ph):
        for p in range(npiece[ph]):
            for dr in (0, 1):
                if has(ph, dr, 1, p):
                    ring_desc(ph, dr, 1, 0, p).start()

    def relay(ph, k, p):
        for dr in (0, 1):
            if not has(ph, dr, k, p):
                continue
            ring_desc(ph, dr, k, k, p).wait_recv()
            if has(ph, dr, k + 1, p):
                ring_desc(ph, dr, k + 1, k, p).start()
            part_desc(ph, dr, k, core, p).start()

    def collect(ph, k):
        for dr in (0, 1):
            for p in range(npiece[ph]):
                if has(ph, dr, k, p):
                    part_desc(ph, dr, k, 1 - core, p).wait_recv()

    def drain(ph, ks):
        for k in ks:
            for dr in (0, 1):
                for p in range(npiece[ph]):
                    if has(ph, dr, k, p):
                        ring_desc(ph, dr, k, k, p).wait_send()
                        part_desc(ph, dr, k, core, p).wait_send()

    order = [d] + [origin(dr, k) for k in range(1, K) for dr in (0, 1)] + [origin(0, K)]

    half = T // 2

    def tok_desc(j):
        rows = pl.ds(j // N * half, half)
        cols = pl.ds(pl.multiple_of(order[j % N] * R, R), R)
        return mk(tok_hbm.at[rows, cols], tokp.at[rows, cols], ts.at[j], tr.at[j], dev(seq=xpeer))

    def blk(b):
        return 2 * (x if b == 0 else 1 - x) + core

    def st_desc(b, i, mine):
        ref = st.at[blk(b) if mine else blk(b) + 1 - 2 * core, i]
        return mk(ref, ref, sts.at[b, i], str_.at[b, i], dev(seq=partner))

    def tot_desc(b, mine):
        ref = tot.at[blk(b) if mine else blk(b) + 1 - 2 * core]
        return mk(ref, ref, tos.at[b], tor.at[b], dev(seq=partner))

    def g_desc(i, h, mine):
        c = (x if mine else 1 - x) * FX + i * hd
        rows = pl.ds(h * half, half)
        return mk(gsend.at[i, rows], gated.at[rows, pl.ds(pl.multiple_of(c, hd), hd)],
                  gs.at[h, i], gr.at[h, i], dev(seq=xpeer))

    ld_copy = mk(ld_hbm, ldp, ls, lr, dev(seq=xpeer))
    ss_copy = mk(ssrow.at[1], ssin, sss, ssr, dev(seq=xpeer))

    def chain_desc(i, to):
        return mk(cout.at[i], cin.at[i], cs.at[i], cr.at[i], dev(seq=to))

    barrier = pltpu.get_barrier_semaphore()
    for who in (dev(dp=ring_to[0]), dev(dp=ring_to[1]), dev(seq=partner), dev(seq=xpeer)):
        pl.semaphore_signal(barrier, inc=1, device_id=who, device_id_type=MESH)
    greeted = 4
    if groups > 1:
        @pl.when(group > 0)
        def _():
            pl.semaphore_signal(barrier, inc=1, device_id=dev(seq=s - 4), device_id_type=MESH)

        @pl.when(group < groups - 1)
        def _():
            pl.semaphore_signal(barrier, inc=1, device_id=dev(seq=s + 4), device_id_type=MESH)
        greeted = greeted + jnp.where(group > 0, 1, 0) + jnp.where(group < groups - 1, 1, 0)
    base = pl.multiple_of(d * R, R)
    loads = []
    for p in range(PARTS):
        src = wgate.at[:, pl.ds(xcol, FX)] if p == 3 else wqkv.at[:, pl.ds(p * F + xcol, FX)]
        loads.append(pltpu.make_async_copy(
            src, W.at[pl.ds(base, R), pl.ds(p * FX, FX)], loc_sem.at[p]))
    loads.append(pltpu.make_async_copy(
        wout, WO.at[pl.ds(pl.multiple_of(d * RO, RO), RO), :], loc_sem.at[4]))
    for c in loads:
        c.start()
    tok_load = pltpu.make_async_copy(tok_hbm, tok, tok_sem)
    tok_load.start()
    small = [pltpu.make_async_copy(ld_hbm, ld, loc_sem.at[5]),
             pltpu.make_async_copy(gain_hbm, gain, loc_sem.at[6])]
    for c in small:
        c.start()

    lane = lax.broadcasted_iota(jnp.int32, (H, T), 1)

    def decays(b, rows):
        cum = rows
        step = 1
        while step < T:
            cum = cum + jnp.where(lane >= step, pltpu.roll(cum, step, 1), 0.0)
            step *= 2
        cums[b] = cum
        for i in range(HX):
            row = cums[b, pl.ds(x * HX + i, 1), :]
            crow[b, i] = jnp.broadcast_to(row, (8, T))
            col = jnp.broadcast_to(row, (hd, T)).T
            ccol[b, i] = col
            tot[blk(b), i:i + 1, :] = col[T - 1:T, :]

    toks = (tok, tokp)
    accs = (acc0, acc1)

    def matmul(b, origins, rs=slice(None), first=False):
        rows = [pl.ds(pl.multiple_of(o * R, R), R) for o in origins]
        left = jnp.concatenate([toks[b][rs, r] for r in rows], axis=1)
        right = jnp.concatenate([W[r, :] for r in rows], axis=0)
        y = jnp.dot(left, right, preferred_element_type=F32)
        if first:
            accs[b][rs, :] = y
        else:
            accs[b][rs, :] += y

    def step_origins(k):
        return [origin(0, k)] if k == K else [origin(0, k), origin(1, k)]

    def silu(v):
        return (v / (1.0 + jnp.exp(-v))).astype(BF16)

    halves = (slice(0, half), slice(half, T))

    def head_local(b, i, r=slice(None)):
        a = accs[b]
        k_s[b, i, r, :] = silu(a[r, FX + i * hd:FX + (i + 1) * hd])
        v_s[b, i, r, :] = silu(a[r, 2 * FX + i * hd:2 * FX + (i + 1) * hd])
        q_s[b, i, r, :] = silu(a[r, i * hd:(i + 1) * hd])

    def head_state(b, i):
        c = ccol[b, i]
        sk = (k_s[b, i].astype(F32) * jnp.exp(c[T - 1:T, :] - c)).astype(BF16)
        st[blk(b), i] = lax.dot_general(sk, v_s[b, i], (((0,), (0,)), ((), ())),
                                        preferred_element_type=F32)
        st_desc(b, i, True).start()

    tri = (lax.broadcasted_iota(jnp.int32, (half, half), 1)
           <= lax.broadcasted_iota(jnp.int32, (half, half), 0))

    def head_attend(b, i, u):
        r = halves[u]
        q = q_s[b, i, r, :]
        c = jnp.concatenate([ccol[b, i, r, :]] * (half // hd), axis=1)
        total = None
        for e in range(u + 1):
            z = halves[e]
            sc = lax.dot_general(q, k_s[b, i, z, :], (((1,), (1,)), ((), ())),
                                 preferred_element_type=F32)
            gap = c - crow[b, i, 0:1, z]
            if e == u:
                gap = jnp.where(tri, gap, -1e30)
            w = (sc * jnp.exp(gap)).astype(BF16)
            y = jnp.dot(w, v_s[b, i, z, :], preferred_element_type=F32)
            total = y if total is None else total + y
        att[b, i, r, :] = total

    def fold(first, count, i):
        def one(j, c):
            return jnp.exp(tot[j, i:i + 1, :]) * c + st[j, i]
        return lax.fori_loop(0, count, one, first)

    def head_final(b, i, h):
        r = halves[h]
        if h == 0:
            car[b, i] = fold(cin[i], blk(b), i).astype(BF16)
        inter = jnp.dot(q_s[b, i, r, :], car[b, i], preferred_element_type=F32)
        a = att[b, i, r, :] + inter * jnp.exp(ccol[b, i, r, :])
        if i == 0:
            ss[b, r, :] = a * a
        else:
            ss[b, r, :] += a * a
        g = accs[b][r, 3 * FX + i * hd:3 * FX + (i + 1) * hd]
        f = pl.ds(pl.multiple_of(x * FX + i * hd, hd), hd)
        val = (a * gain[:, f] * (1.0 / (1.0 + jnp.exp(-g)))).astype(BF16)
        if b == 0:
            gated[r, f] = val
        else:
            gsend[i, r, :] = val
            g_desc(i, h, True).start()

    def row_sums(b):
        ssrow[b] = jnp.broadcast_to(jnp.sum(ss[b].T, axis=0, keepdims=True), (8, T))

    if groups == 1:
        cin[...] = jnp.zeros_like(cin)
    else:
        @pl.when(group == 0)
        def _():
            cin[...] = jnp.zeros_like(cin)

    def chain(i):
        if groups == 1:
            return

        @pl.when(group > 0)
        def _():
            chain_desc(i, s - 4).wait_recv()

        @pl.when(group < groups - 1)
        def _():
            cout[i] = fold(cin[i], 4, i)
            chain_desc(i, s + 4).start()

    pl.semaphore_wait(barrier, greeted)
    begin(0)
    started = [0]
    total_toks = 2 * N

    def tok_next():
        j = started[0]
        if j < total_toks:
            if j >= WINDOW:
                tok_desc(j - WINDOW).wait_send()
            tok_desc(j).start()
            started[0] = j + 1

    def tok_need(j):
        while started[0] <= min(j + WINDOW - 1, total_toks - 1):
            tok_next()
        tok_desc(j).wait_recv()

    for _ in range(WINDOW):
        tok_next()
    ld_copy.start()
    for c in small:
        c.wait()
    decays(0, ld[...])
    tot_desc(0, True).start()
    for c in loads:
        c.wait()
    tok_load.wait()
    matmul(0, [d], first=True)

    def peer_step(h, k):
        for j in ([0] if k == 0 else range(2 * k - 1, min(2 * k + 1, N))):
            tok_need(h * N + j)
        matmul(1, [d] if k == 0 else step_origins(k), halves[h], k == 0)

    late = [0]
    wo = ([(k, p) for k in range(1, K) for p in range(OPIECES)]
          + [(K, p) for a in range(OPIECES // 2) for p in (a, a + OPIECES // 2)])

    def wo_next(n=1):
        for _ in range(n):
            if wo:
                k, p = wo.pop(0)
                relay(1, k, p)
                if k == K:
                    relay(1, *wo.pop(0))

    for k in range(1, K):
        relay(0, k, 0)
        tok_next()
        if k > 1:
            collect(0, k - 1)
            matmul(0, step_origins(k - 1))
        relay(0, k, 1)
        tok_next()
        if k == 1:
            ld_copy.wait_recv()
            decays(1, ldp[...])
            tot_desc(1, True).start()
        peer_step(0, k - 1)
        relay(0, k, 2)
        tok_next()
        relay(0, k, 3)
        tok_next()
        while N + 2 * late[0] <= 4 * k - 2:
            peer_step(1, late[0])
            late[0] += 1
    begin(1)
    relay(0, K, 0)
    relay(0, K, 2)
    tok_next()
    collect(0, K - 1)
    matmul(0, step_origins(K - 1))
    peer_step(0, K - 1)
    relay(0, K, 1)
    relay(0, K, 3)
    tok_next()
    while late[0] < K - 1:
        peer_step(1, late[0])
        late[0] += 1
    collect(0, K)
    matmul(0, step_origins(K))
    peer_step(0, K)
    def relay_at(point):
        wo_next(PLAN.count(point))

    for i in range(HX):
        head_local(0, i)
        head_state(0, i)
        if i == 1:
            relay_at("B")
    for b in (0, 1):
        tot_desc(b, False).wait_recv()
    relay_at("C")
    for i in range(HX):
        head_local(1, i, halves[0])
        head_attend(1, i, 0)
        if i == 1:
            relay_at("D")
    relay_at("E")
    for i in range(HX):
        st_desc(0, i, False).wait_recv()
    early = groups == 1
    if early:
        @pl.when(core == 0)
        def _():
            for i in range(HX):
                head_final(1, i, 0)
    relay_at("F")
    while late[0] <= K:
        peer_step(1, late[0])
        late[0] += 1
        relay_at("G" if late[0] <= K else "H")
    for i in range(HX):
        head_local(1, i, halves[1])
        head_state(1, i)
        if i == 1:
            relay_at("I")
    relay_at("J")
    head_attend(1, 0, 1)
    for i in range(HX):
        st_desc(1, i, False).wait_recv()
        chain(i)
    if early:
        @pl.when(core == 1)
        def _():
            for i in range(HX):
                head_final(1, i, 0)
    else:
        for i in range(HX):
            head_final(1, i, 0)
    relay_at("K")
    for i in range(HX):
        if i:
            head_attend(1, i, 1)
        head_final(1, i, 1)
        if i == 1:
            relay_at("L")
    row_sums(1)
    ss_copy.start()
    relay_at("M")
    for i in range(HX):
        for h in (0, 1):
            head_attend(0, i, h)
            head_final(0, i, h)
        relay_at("NOPQ"[i % 4])
    row_sums(0)
    while wo and wo[0][0] < K:
        wo_next()
    for k in range(1, K):
        collect(1, k)
    drain(0, range(1, K + 1))
    for j in range(total_toks - WINDOW, total_toks):
        tok_desc(j).wait_send()
    ld_copy.wait_send()
    for b in (0, 1):
        tot_desc(b, True).wait_send()
        for i in range(HX):
            st_desc(b, i, True).wait_send()
    ss_copy.wait_recv()
    inv = lax.rsqrt((ssrow[0, 0:1, :] + ssin[0:1, :]) * (1.0 / F) + 1e-06)
    ss[0] = jnp.broadcast_to(inv, (hd, T)).T
    for i in range(HX):
        for h in (0, 1):
            g_desc(i, h, False).wait_recv()

    split = RO % 128 == 0
    last = order[-1:] if split else []
    done = order[:-1] if split else []

    def mix(origins, cols):
        at = [pl.ds(pl.multiple_of(o * RO, RO), RO) for o in origins]
        left = jnp.concatenate([gated[:, r] for r in at], axis=1)
        right = jnp.concatenate([WO[r, cols] for r in at], axis=0)
        return jnp.dot(left, right, preferred_element_type=F32)

    for u in range(4):
        cols = slice(u * D // 4, (u + 1) * D // 4)
        if split:
            part[:, cols] = mix(done, cols)
        if u in (0, 1):
            wo_next()
    while wo:
        wo_next()
    scale[...] = ss[0]
    drain(1, range(1, K))
    collect(1, K)
    if split:
        gz[...] = gated[:, pl.ds(pl.multiple_of(last[0] * RO, RO), RO)]
        wz[...] = WO[pl.ds(pl.multiple_of(last[0] * RO, RO), RO), :]
    else:
        part[...] = jnp.dot(gated[...], WO[...], preferred_element_type=F32)
        gz[...] = jnp.zeros_like(gz)
        wz[...] = jnp.zeros_like(wz)

    drain(1, range(K, K + 1))
    for i in range(HX):
        for h in (0, 1):
            g_desc(i, h, True).wait_send()
    ss_copy.wait_send()
    if groups > 1:
        @pl.when(group < groups - 1)
        def _():
            for i in range(HX):
                chain_desc(i, s + 4).wait_send()


def finish(part, gz, wz, scale, out, ob, sem):
    D = part.shape[1]
    width = D // 4
    copies = []
    for u in range(4):
        cols = slice(u * width, (u + 1) * width)
        y = part[:, cols] + jnp.dot(gz[...], wz[:, cols], preferred_element_type=F32)
        wide = jnp.concatenate([scale[...]] * (width // scale.shape[1]), axis=1)
        ob[:, cols] = (y * wide).astype(BF16)
        c = pltpu.make_async_copy(ob.at[:, cols], out.at[:, cols], sem.at[u])
        c.start()
        copies.append(c)
    for c in copies:
        c.wait()


def body(n_dp, n_seq, tokens, log_decay, w_qkv, w_gate, w_out, norm_gain):
    tok = tokens[0]
    T, D = tok.shape
    H = log_decay.shape[1]
    F = norm_gain.shape[0]
    hd = F // H
    HX = H // 2
    vm = pl.BlockSpec(memory_space=pltpu.VMEM)
    hbm = pl.BlockSpec(memory_space=pl.ANY)
    dma = pltpu.SemaphoreType.DMA
    V = pltpu.VMEM
    m = n_dp // 2
    RO = F // n_dp
    parts = pl.pallas_call(
        functools.partial(fused, n_dp, n_seq),
        out_shape=(V((T, D), F32), V((T, RO), BF16), V((RO, D), BF16), V((T, hd), F32)),
        in_specs=[hbm] * 6,
        out_specs=(vm, vm, vm, vm),
        scratch_shapes=[
            V((T, D), BF16), V((T, D), BF16), V((H, T), F32), V((1, F), F32), V((D, 2 * F), BF16), V((F, D), BF16),
            V((T, 2 * F), F32), V((T, 2 * F), F32),
            V((2, HX, T, hd), BF16), V((2, HX, T, hd), BF16), V((2, HX, T, hd), BF16),
            V((2, HX, T, hd), F32), V((2, HX, T, hd), F32), V((2, HX, 8, T), F32),
            V((2, H, T), F32), V((H, T), F32), V((4, 8, hd), F32), V((4, HX, hd, hd), F32),
            V((HX, hd, hd), F32), V((HX, hd, hd), F32),
            V((2, T, hd), F32), V((2, 8, T), F32), V((8, T), F32), V((T, F), BF16),
            V((HX, T, hd), BF16), V((2, HX, hd, hd), BF16),
            dma((7,)), dma,
            dma((2, WPIECES, m)), dma((2, WPIECES, m)), dma((2, WPIECES, m)), dma((2, WPIECES, m)),
            dma((2, OPIECES, m)), dma((2, OPIECES, m)), dma((2, OPIECES, m)), dma((2, OPIECES, m)),
            dma((2 * n_dp,)), dma((2 * n_dp,)), dma, dma, dma((2,)), dma((2,)),
            dma((2, HX)), dma((2, HX)), dma((2, HX)), dma((2, HX)), dma, dma, dma((HX,)), dma((HX,)),
        ],
        compiler_params=pltpu.CompilerParams(
            collective_id=0, has_side_effects=True, vmem_limit_bytes=57 * 1024 * 1024),
    )(tok, log_decay[0], norm_gain[None], w_qkv, w_gate, w_out)
    y = pl.pallas_call(
        finish,
        out_shape=jax.ShapeDtypeStruct((T, D), BF16),
        in_specs=[vm] * 4,
        out_specs=hbm,
        scratch_shapes=[V((T, D), BF16), dma((4,))],
        compiler_params=pltpu.CompilerParams(vmem_limit_bytes=8 * 1024 * 1024),
    )(*[pltpu.with_memory_space_constraint(a, pltpu.VMEM) for a in parts])
    return y[None]


def solution(mesh):
    placed = (
        P("dp", "seq", None),
        P("dp", None, "seq"),
        P("dp", None),
        P("dp", None),
        P("dp", None),
        P(),
    )
    return jax.shard_map(
        functools.partial(body, mesh.shape["dp"], mesh.shape["seq"]),
        mesh=mesh, in_specs=placed, out_specs=P("dp", "seq", None), check_vma=False
    )
```

```python
import functools

import jax
import jax.numpy as jnp
from jax import lax
from jax.experimental import pallas as pl
from jax.experimental.pallas import tpu as pltpu
from jax.sharding import PartitionSpec as P

MESH = pl.DeviceIdType.MESH
F32 = jnp.float32
BF16 = jnp.bfloat16
PARTS = 4
WPIECES = 4
OPIECES = 4
WINDOW = 2
PLAN = "CEFHJKMOQ"


def fused(n_dp, n_seq, tok_hbm, ld_hbm, gain_hbm, wqkv, wgate, wout, part, gz, wz, scale,
          tok, tokp, ld, gain, W, WO, acc0, acc1, q_s, k_s, v_s, att, ccol, crow, cums, ldp, tot, st, cin,
          cout, ss, ssrow, ssin, gated, gsend, car,
          loc_sem, tok_sem, wr, ws, wpr, wps, orr, ors, opr, ops, tr, ts, lr, ls, tor, tos,
          str_, sts, gr, gs, ssr, sss, cr, cs):
    T, D = tok_hbm.shape
    H = ld_hbm.shape[0]
    F = gain_hbm.shape[1]
    hd = F // H
    HX = H // 2
    FX = F // 2
    N = n_dp
    K = N // 2
    R = D // N
    RO = F // N
    groups = n_seq // 4
    s = lax.axis_index("seq")
    d = lax.axis_index("dp")
    core = s % 2
    x = (s // 2) % 2
    group = s // 4
    partner = s + 1 - 2 * core
    xpeer = s + 2 - 4 * x

    def pos_of(i):
        return jnp.where(i % 2 == 0, i // 2, N - 1 - i // 2)

    def dev_at(p):
        p = lax.rem(p + 2 * N, N)
        return jnp.where(p < K, 2 * p, 2 * (N - 1 - p) + 1)

    pos = pos_of(d)
    ring_to = (dev_at(pos + 1), dev_at(pos - 1))

    def origin(dr, k):
        return dev_at(pos - k) if dr == 0 else dev_at(pos + k)

    def dev(seq=None, dp=None):
        return {"seq": s if seq is None else seq, "dp": d if dp is None else dp}

    def mk(src, dst, ssem, rsem, to):
        return pltpu.make_async_remote_copy(
            src_ref=src, dst_ref=dst, send_sem=ssem, recv_sem=rsem,
            device_id=to, device_id_type=MESH)

    npiece = (WPIECES, OPIECES)
    ring_sems = ((ws, wr, wps, wpr), (ors, orr, ops, opr))

    def piece(ph, dr, k, c, p):
        rows, buf = ((R, W), (RO, WO))[ph]
        width = buf.shape[1] // npiece[ph]
        q = rows // 2
        row = pl.multiple_of(origin(dr, k) * rows + c * q, q)
        return buf.at[pl.ds(row, q), pl.ds(p * width, width)]

    xcol = pl.multiple_of(x * FX, FX)

    def own(ph, p):
        q = (R, RO)[ph] // 2
        rows = pl.ds(pl.multiple_of(core * q, q), q)
        if ph == 1:
            width = D // OPIECES
            return wout.at[rows, pl.ds(p * width, width)]
        if p == 3:
            return wgate.at[rows, pl.ds(xcol, FX)]
        return wqkv.at[rows, pl.ds(p * F + xcol, FX)]

    def has(ph, dr, k, p):
        return k < K or (k == K and (p * 2) // npiece[ph] == dr)

    def ring_desc(ph, dr, k, at, p):
        a, b = ring_sems[ph][:2]
        ref = piece(ph, dr, at, core, p)
        return mk(ref if at else own(ph, p), ref, a.at[dr, p, k - 1], b.at[dr, p, k - 1],
                  dev(dp=ring_to[dr]))

    def part_desc(ph, dr, k, c, p):
        a, b = ring_sems[ph][2:]
        ref = piece(ph, dr, k, c, p)
        return mk(ref, ref, a.at[dr, p, k - 1], b.at[dr, p, k - 1], dev(seq=partner))

    def begin(ph):
        for p in range(npiece[ph]):
            for dr in (0, 1):
                if has(ph, dr, 1, p):
                    ring_desc(ph, dr, 1, 0, p).start()

    def relay(ph, k, p):
        for dr in (0, 1):
            if not has(ph, dr, k, p):
                continue
            ring_desc(ph, dr, k, k, p).wait_recv()
            if has(ph, dr, k + 1, p):
                ring_desc(ph, dr, k + 1, k, p).start()
            part_desc(ph, dr, k, core, p).start()

    def collect(ph, k):
        for dr in (0, 1):
            for p in range(npiece[ph]):
                if has(ph, dr, k, p):
                    part_desc(ph, dr, k, 1 - core, p).wait_recv()

    def drain(ph, ks):
        for k in ks:
            for dr in (0, 1):
                for p in range(npiece[ph]):
                    if has(ph, dr, k, p):
                        ring_desc(ph, dr, k, k, p).wait_send()
                        part_desc(ph, dr, k, core, p).wait_send()

    order = [d] + [origin(dr, k) for k in range(1, K) for dr in (0, 1)] + [origin(0, K)]

    half = T // 2

    def tok_desc(j):
        rows = pl.ds(j // N * half, half)
        cols = pl.ds(pl.multiple_of(order[j % N] * R, R), R)
        return mk(tok_hbm.at[rows, cols], tokp.at[rows, cols], ts.at[j], tr.at[j], dev(seq=xpeer))

    def blk(b):
        return 2 * (x if b == 0 else 1 - x) + core

    def st_desc(b, i, mine):
        ref = st.at[blk(b) if mine else blk(b) + 1 - 2 * core, i]
        return mk(ref, ref, sts.at[b, i], str_.at[b, i], dev(seq=partner))

    def tot_desc(b, mine):
        ref = tot.at[blk(b) if mine else blk(b) + 1 - 2 * core]
        return mk(ref, ref, tos.at[b], tor.at[b], dev(seq=partner))

    def g_desc(i, h, mine):
        c = (x if mine else 1 - x) * FX + i * hd
        rows = pl.ds(h * half, half)
        return mk(gsend.at[i, rows], gated.at[rows, pl.ds(pl.multiple_of(c, hd), hd)],
                  gs.at[h, i], gr.at[h, i], dev(seq=xpeer))

    ld_copy = mk(ld_hbm, ldp, ls, lr, dev(seq=xpeer))
    ss_copy = mk(ssrow.at[1], ssin, sss, ssr, dev(seq=xpeer))

    def chain_desc(i, to):
        return mk(cout.at[i], cin.at[i], cs.at[i], cr.at[i], dev(seq=to))

    barrier = pltpu.get_barrier_semaphore()
    for who in (dev(dp=ring_to[0]), dev(dp=ring_to[1]), dev(seq=partner), dev(seq=xpeer)):
        pl.semaphore_signal(barrier, inc=1, device_id=who, device_id_type=MESH)
    greeted = 4
    if groups > 1:
        @pl.when(group > 0)
        def _():
            pl.semaphore_signal(barrier, inc=1, device_id=dev(seq=s - 4), device_id_type=MESH)

        @pl.when(group < groups - 1)
        def _():
            pl.semaphore_signal(barrier, inc=1, device_id=dev(seq=s + 4), device_id_type=MESH)
        greeted = greeted + jnp.where(group > 0, 1, 0) + jnp.where(group < groups - 1, 1, 0)
    base = pl.multiple_of(d * R, R)
    loads = []
    for p in range(PARTS):
        src = wgate.at[:, pl.ds(xcol, FX)] if p == 3 else wqkv.at[:, pl.ds(p * F + xcol, FX)]
        loads.append(pltpu.make_async_copy(
            src, W.at[pl.ds(base, R), pl.ds(p * FX, FX)], loc_sem.at[p]))
    loads.append(pltpu.make_async_copy(
        wout, WO.at[pl.ds(pl.multiple_of(d * RO, RO), RO), :], loc_sem.at[4]))
    for c in loads:
        c.start()
    tok_load = pltpu.make_async_copy(tok_hbm, tok, tok_sem)
    tok_load.start()
    small = [pltpu.make_async_copy(ld_hbm, ld, loc_sem.at[5]),
             pltpu.make_async_copy(gain_hbm, gain, loc_sem.at[6])]
    for c in small:
        c.start()

    lane = lax.broadcasted_iota(jnp.int32, (H, T), 1)

    def decays(b, rows):
        cum = rows
        step = 1
        while step < T:
            cum = cum + jnp.where(lane >= step, pltpu.roll(cum, step, 1), 0.0)
            step *= 2
        cums[b] = cum
        for i in range(HX):
            row = cums[b, pl.ds(x * HX + i, 1), :]
            crow[b, i] = jnp.broadcast_to(row, (8, T))
            col = jnp.broadcast_to(row, (hd, T)).T
            ccol[b, i] = col
            tot[blk(b), i:i + 1, :] = col[T - 1:T, :]

    toks = (tok, tokp)
    accs = (acc0, acc1)

    def matmul(b, origins, rs=slice(None), first=False):
        rows = [pl.ds(pl.multiple_of(o * R, R), R) for o in origins]
        left = jnp.concatenate([toks[b][rs, r] for r in rows], axis=1)
        right = jnp.concatenate([W[r, :] for r in rows], axis=0)
        y = jnp.dot(left, right, preferred_element_type=F32)
        if first:
            accs[b][rs, :] = y
        else:
            accs[b][rs, :] += y

    def step_origins(k):
        return [origin(0, k)] if k == K else [origin(0, k), origin(1, k)]

    def silu(v):
        return (v / (1.0 + jnp.exp(-v))).astype(BF16)

    halves = (slice(0, half), slice(half, T))

    def head_local(b, i, r=slice(None)):
        a = accs[b]
        k_s[b, i, r, :] = silu(a[r, FX + i * hd:FX + (i + 1) * hd])
        v_s[b, i, r, :] = silu(a[r, 2 * FX + i * hd:2 * FX + (i + 1) * hd])
        q_s[b, i, r, :] = silu(a[r, i * hd:(i + 1) * hd])

    def head_state(b, i):
        c = ccol[b, i]
        sk = (k_s[b, i].astype(F32) * jnp.exp(c[T - 1:T, :] - c)).astype(BF16)
        st[blk(b), i] = lax.dot_general(sk, v_s[b, i], (((0,), (0,)), ((), ())),
                                        preferred_element_type=F32)
        st_desc(b, i, True).start()

    tri = (lax.broadcasted_iota(jnp.int32, (half, half), 1)
           <= lax.broadcasted_iota(jnp.int32, (half, half), 0))

    def head_attend(b, i, u):
        r = halves[u]
        q = q_s[b, i, r, :]
        c = jnp.concatenate([ccol[b, i, r, :]] * (half // hd), axis=1)
        total = None
        for e in range(u + 1):
            z = halves[e]
            sc = lax.dot_general(q, k_s[b, i, z, :], (((1,), (1,)), ((), ())),
                                 preferred_element_type=F32)
            gap = c - crow[b, i, 0:1, z]
            if e == u:
                gap = jnp.where(tri, gap, -1e30)
            w = (sc * jnp.exp(gap)).astype(BF16)
            y = jnp.dot(w, v_s[b, i, z, :], preferred_element_type=F32)
            total = y if total is None else total + y
        att[b, i, r, :] = total

    def fold(first, count, i):
        def one(j, c):
            return jnp.exp(tot[j, i:i + 1, :]) * c + st[j, i]
        return lax.fori_loop(0, count, one, first)

    def head_final(b, i, h):
        r = halves[h]
        if h == 0:
            car[b, i] = fold(cin[i], blk(b), i).astype(BF16)
        inter = jnp.dot(q_s[b, i, r, :], car[b, i], preferred_element_type=F32)
        a = att[b, i, r, :] + inter * jnp.exp(ccol[b, i, r, :])
        if i == 0:
            ss[b, r, :] = a * a
        else:
            ss[b, r, :] += a * a
        g = accs[b][r, 3 * FX + i * hd:3 * FX + (i + 1) * hd]
        f = pl.ds(pl.multiple_of(x * FX + i * hd, hd), hd)
        val = (a * gain[:, f] * (1.0 / (1.0 + jnp.exp(-g)))).astype(BF16)
        if b == 0:
            gated[r, f] = val
        else:
            gsend[i, r, :] = val
            g_desc(i, h, True).start()

    def row_sums(b):
        ssrow[b] = jnp.broadcast_to(jnp.sum(ss[b].T, axis=0, keepdims=True), (8, T))

    if groups == 1:
        cin[...] = jnp.zeros_like(cin)
    else:
        @pl.when(group == 0)
        def _():
            cin[...] = jnp.zeros_like(cin)

    def chain(i):
        if groups == 1:
            return

        @pl.when(group > 0)
        def _():
            chain_desc(i, s - 4).wait_recv()

        @pl.when(group < groups - 1)
        def _():
            cout[i] = fold(cin[i], 4, i)
            chain_desc(i, s + 4).start()

    pl.semaphore_wait(barrier, greeted)
    begin(0)
    started = [0]
    total_toks = 2 * N

    def tok_next():
        j = started[0]
        if j < total_toks:
            if j >= WINDOW:
                tok_desc(j - WINDOW).wait_send()
            tok_desc(j).start()
            started[0] = j + 1

    def tok_need(j):
        while started[0] <= min(j + WINDOW - 1, total_toks - 1):
            tok_next()
        tok_desc(j).wait_recv()

    for _ in range(WINDOW):
        tok_next()
    ld_copy.start()
    for c in small:
        c.wait()
    decays(0, ld[...])
    tot_desc(0, True).start()
    for c in loads:
        c.wait()
    tok_load.wait()
    matmul(0, [d], first=True)

    def peer_step(h, k):
        for j in ([0] if k == 0 else range(2 * k - 1, min(2 * k + 1, N))):
            tok_need(h * N + j)
        matmul(1, [d] if k == 0 else step_origins(k), halves[h], k == 0)

    late = [0]
    wo = ([(k, p) for k in range(1, K) for p in range(OPIECES)]
          + [(K, p) for a in range(OPIECES // 2) for p in (a, a + OPIECES // 2)])

    def wo_next(n=1):
        for _ in range(n):
            if wo:
                k, p = wo.pop(0)
                relay(1, k, p)
                if k == K:
                    relay(1, *wo.pop(0))

    for k in range(1, K):
        relay(0, k, 0)
        tok_next()
        if k > 1:
            collect(0, k - 1)
            matmul(0, step_origins(k - 1))
        relay(0, k, 1)
        tok_next()
        if k == 1:
            ld_copy.wait_recv()
            decays(1, ldp[...])
            tot_desc(1, True).start()
        peer_step(0, k - 1)
        relay(0, k, 2)
        tok_next()
        relay(0, k, 3)
        tok_next()
        while N + 2 * late[0] <= 4 * k - 2:
            peer_step(1, late[0])
            late[0] += 1
    begin(1)
    relay(0, K, 0)
    relay(0, K, 2)
    tok_next()
    collect(0, K - 1)
    matmul(0, step_origins(K - 1))
    peer_step(0, K - 1)
    relay(0, K, 1)
    relay(0, K, 3)
    tok_next()
    while late[0] < K - 1:
        peer_step(1, late[0])
        late[0] += 1
    collect(0, K)
    matmul(0, step_origins(K))
    peer_step(0, K)
    def relay_at(point):
        wo_next(PLAN.count(point))

    for i in range(HX):
        head_local(0, i)
        head_state(0, i)
        if i == 1:
            relay_at("B")
    for b in (0, 1):
        tot_desc(b, False).wait_recv()
    relay_at("C")
    for i in range(HX):
        head_local(1, i, halves[0])
        head_attend(1, i, 0)
        if i == 1:
            relay_at("D")
    relay_at("E")
    for i in range(HX):
        st_desc(0, i, False).wait_recv()
    early = groups == 1
    if early:
        @pl.when(core == 0)
        def _():
            for i in range(HX):
                head_final(1, i, 0)
    relay_at("F")
    while late[0] <= K:
        peer_step(1, late[0])
        late[0] += 1
        relay_at("G" if late[0] <= K else "H")
    for i in range(HX):
        head_local(1, i, halves[1])
        head_state(1, i)
        if i == 1:
            relay_at("I")
    relay_at("J")
    head_attend(1, 0, 1)
    for i in range(HX):
        st_desc(1, i, False).wait_recv()
        chain(i)
    if early:
        @pl.when(core == 1)
        def _():
            for i in range(HX):
                head_final(1, i, 0)
    else:
        for i in range(HX):
            head_final(1, i, 0)
    relay_at("K")
    for i in range(HX):
        if i:
            head_attend(1, i, 1)
        head_final(1, i, 1)
        if i == 1:
            relay_at("L")
    row_sums(1)
    ss_copy.start()
    relay_at("M")
    for i in range(HX):
        for h in (0, 1):
            head_attend(0, i, h)
            head_final(0, i, h)
        relay_at("NOPQ"[i % 4])
    row_sums(0)
    while wo and wo[0][0] < K:
        wo_next()
    for k in range(1, K):
        collect(1, k)
    drain(0, range(1, K + 1))
    for j in range(total_toks - WINDOW, total_toks):
        tok_desc(j).wait_send()
    ld_copy.wait_send()
    for b in (0, 1):
        tot_desc(b, True).wait_send()
        for i in range(HX):
            st_desc(b, i, True).wait_send()
    ss_copy.wait_recv()
    inv = lax.rsqrt((ssrow[0, 0:1, :] + ssin[0:1, :]) * (1.0 / F) + 1e-06)
    ss[0] = jnp.broadcast_to(inv, (hd, T)).T
    for i in range(HX):
        for h in (0, 1):
            g_desc(i, h, False).wait_recv()

    split = RO % 128 == 0
    last = order[-1:] if split else []
    done = order[:-1] if split else []

    def mix(origins, cols):
        at = [pl.ds(pl.multiple_of(o * RO, RO), RO) for o in origins]
        left = jnp.concatenate([gated[:, r] for r in at], axis=1)
        right = jnp.concatenate([WO[r, cols] for r in at], axis=0)
        return jnp.dot(left, right, preferred_element_type=F32)

    for u in range(4):
        cols = slice(u * D // 4, (u + 1) * D // 4)
        if split:
            part[:, cols] = mix(done, cols)
        if u in (0, 1):
            wo_next()
    while wo:
        wo_next()
    scale[...] = ss[0]
    drain(1, range(1, K))
    collect(1, K)
    if split:
        gz[...] = gated[:, pl.ds(pl.multiple_of(last[0] * RO, RO), RO)]
        wz[...] = WO[pl.ds(pl.multiple_of(last[0] * RO, RO), RO), :]
    else:
        part[...] = jnp.dot(gated[...], WO[...], preferred_element_type=F32)
        gz[...] = jnp.zeros_like(gz)
        wz[...] = jnp.zeros_like(wz)

    drain(1, range(K, K + 1))
    for i in range(HX):
        for h in (0, 1):
            g_desc(i, h, True).wait_send()
    ss_copy.wait_send()
    if groups > 1:
        @pl.when(group < groups - 1)
        def _():
            for i in range(HX):
                chain_desc(i, s + 4).wait_send()


def finish(part, gz, wz, scale, out, ob, sem):
    D = part.shape[1]
    width = D // 4
    copies = []
    for u in range(4):
        cols = slice(u * width, (u + 1) * width)
        y = part[:, cols] + jnp.dot(gz[...], wz[:, cols], preferred_element_type=F32)
        wide = jnp.concatenate([scale[...]] * (width // scale.shape[1]), axis=1)
        ob[:, cols] = (y * wide).astype(BF16)
        c = pltpu.make_async_copy(ob.at[:, cols], out.at[:, cols], sem.at[u])
        c.start()
        copies.append(c)
    for c in copies:
        c.wait()


def body(n_dp, n_seq, tokens, log_decay, w_qkv, w_gate, w_out, norm_gain):
    tok = tokens[0]
    T, D = tok.shape
    H = log_decay.shape[1]
    F = norm_gain.shape[0]
    hd = F // H
    HX = H // 2
    vm = pl.BlockSpec(memory_space=pltpu.VMEM)
    hbm = pl.BlockSpec(memory_space=pl.ANY)
    dma = pltpu.SemaphoreType.DMA
    V = pltpu.VMEM
    m = n_dp // 2
    RO = F // n_dp
    parts = pl.pallas_call(
        functools.partial(fused, n_dp, n_seq),
        out_shape=(V((T, D), F32), V((T, RO), BF16), V((RO, D), BF16), V((T, hd), F32)),
        in_specs=[hbm] * 6,
        out_specs=(vm, vm, vm, vm),
        scratch_shapes=[
            V((T, D), BF16), V((T, D), BF16), V((H, T), F32), V((1, F), F32), V((D, 2 * F), BF16), V((F, D), BF16),
            V((T, 2 * F), F32), V((T, 2 * F), F32),
            V((2, HX, T, hd), BF16), V((2, HX, T, hd), BF16), V((2, HX, T, hd), BF16),
            V((2, HX, T, hd), F32), V((2, HX, T, hd), F32), V((2, HX, 8, T), F32),
            V((2, H, T), F32), V((H, T), F32), V((4, 8, hd), F32), V((4, HX, hd, hd), F32),
            V((HX, hd, hd), F32), V((HX, hd, hd), F32),
            V((2, T, hd), F32), V((2, 8, T), F32), V((8, T), F32), V((T, F), BF16),
            V((HX, T, hd), BF16), V((2, HX, hd, hd), BF16),
            dma((7,)), dma,
            dma((2, WPIECES, m)), dma((2, WPIECES, m)), dma((2, WPIECES, m)), dma((2, WPIECES, m)),
            dma((2, OPIECES, m)), dma((2, OPIECES, m)), dma((2, OPIECES, m)), dma((2, OPIECES, m)),
            dma((2 * n_dp,)), dma((2 * n_dp,)), dma, dma, dma((2,)), dma((2,)),
            dma((2, HX)), dma((2, HX)), dma((2, HX)), dma((2, HX)), dma, dma, dma((HX,)), dma((HX,)),
        ],
        compiler_params=pltpu.CompilerParams(
            collective_id=0, has_side_effects=True, vmem_limit_bytes=57 * 1024 * 1024),
    )(tok, log_decay[0], norm_gain[None], w_qkv, w_gate, w_out)
    y = pl.pallas_call(
        finish,
        out_shape=jax.ShapeDtypeStruct((T, D), BF16),
        in_specs=[vm] * 4,
        out_specs=hbm,
        scratch_shapes=[V((T, D), BF16), dma((4,))],
        compiler_params=pltpu.CompilerParams(vmem_limit_bytes=8 * 1024 * 1024),
    )(*[pltpu.with_memory_space_constraint(a, pltpu.VMEM) for a in parts])
    return y[None]


def solution(mesh):
    placed = (
        P("dp", "seq", None),
        P("dp", None, "seq"),
        P("dp", None),
        P("dp", None),
        P("dp", None),
        P(),
    )
    return jax.shard_map(
        functools.partial(body, mesh.shape["dp"], mesh.shape["seq"]),
        mesh=mesh, in_specs=placed, out_specs=P("dp", "seq", None), check_vma=False
    )
```
